32 devices in a mesh: dp: 4 (over z), fsdp: 8 (over y, x, core).
Axes of the slice: x: 2, y: 2, z: 4, core: 2. Of those that a mesh axis runs over, the one named last changes fastest.
Arguments:
- tokens: bfloat16 [64, 512, 768], P(('dp', 'fsdp')), may hold values from -6 to 6
- lengths: int32 [64], P(('dp', 'fsdp')), may hold values from 40 to 512, as said below
- query_weight: bfloat16 [768, 384], P(('dp', 'fsdp')), may hold values from -0.4375 to 0.4375
- key_weight: bfloat16 [768, 384], P(('dp', 'fsdp')), may hold values from -0.21875 to 0.21875
- value_weight: bfloat16 [768, 384], P(('dp', 'fsdp')), may hold values from -0.21875 to 0.21875
- depth_weight: bfloat16 [9, 768], P(None, ('dp', 'fsdp')), may hold values from -2 to 2
- point_weight: bfloat16 [768, 384], P(('dp', 'fsdp')), may hold values from -0.21875 to 0.21875
- taps_weight: bfloat16 [20736], P(('dp', 'fsdp')), may hold values from -0.3125 to 0.3125
- span_weight: bfloat16 [768, 384], P(('dp', 'fsdp')), may hold values from -0.21875 to 0.21875
- output_weight: bfloat16 [768, 768], P(('dp', 'fsdp')), may hold values from -0.4375 to 0.4375
- scaling: bfloat16 [768], P(('dp', 'fsdp')), may hold values from 0.5 to 1.5
- offsets: bfloat16 [768], P(('dp', 'fsdp')), may hold values from -3 to 3
- inner_weight: bfloat16 [2, 384, 1536], P(None, None, ('dp', 'fsdp')), may hold values from -0.3125 to 0.3125
- outer_weight: bfloat16 [2, 1536, 384], P(None, ('dp', 'fsdp')), may hold values from -0.15625 to 0.15625
- stretch: bfloat16 [768], P(('dp', 'fsdp')), may hold values from 0.5 to 1.5
- displace: bfloat16 [768], P(('dp', 'fsdp')), may hold values from -3 to 3
- cotangent: bfloat16 [64, 512, 768], P(('dp', 'fsdp')), may hold values from -6 to 6
Outputs:
- activations: bfloat16 [64, 512, 768], P(('dp', 'fsdp'))
- tokens_grad: float32 [64, 512, 768], P(('dp', 'fsdp'))
- query_grad: float32 [768, 384], P(('dp', 'fsdp'))
- key_grad: float32 [768, 384], P(('dp', 'fsdp'))
- value_grad: float32 [768, 384], P(('dp', 'fsdp'))
- depth_grad: float32 [9, 768], P(None, ('dp', 'fsdp'))
- point_grad: float32 [768, 384], P(('dp', 'fsdp'))
- taps_grad: float32 [20736], P(('dp', 'fsdp'))
- span_grad: float32 [768, 384], P(('dp', 'fsdp'))
- output_grad: float32 [768, 768], P(('dp', 'fsdp'))
- scaling_grad: float32 [768], P(('dp', 'fsdp'))
- offsets_grad: float32 [768], P(('dp', 'fsdp'))
- inner_grad: float32 [2, 384, 1536], P(None, None, ('dp', 'fsdp'))
- outer_grad: float32 [2, 1536, 384], P(None, ('dp', 'fsdp'))
- stretch_grad: float32 [768], P(('dp', 'fsdp'))
- displace_grad: float32 [768], P(('dp', 'fsdp'))
The draws below stay inside these ranges and needn't reach their ends.
Inputs may be any that keep to these rules, and one draw needn't show every extreme that they name: Sequence i holds lengths[i] real tokens in the first rows of its slot of 512 rows; the rest is padding.
All inputs are finite; a program needn't handle non-finite values.
Results may differ from the reference program's by a relative error of at most 0.012.
The reference program's roundings to bfloat16 on the way count: a program that leaves them out, or rounds other values in their place, can miss the bound.
Values may be sent and summed in bfloat16 or wider, within the bound.
No kernel may reach another device: no remote copies, remote signals or barrier semaphores. Data moves between devices by JAX's collectives and lax.ppermute only.
A program may use at most 192 MiB of HBM per device.

```python
import math
import jax
import jax.numpy as jnp
from jax import lax

D = 768
HEADS = 6
HEAD = 64
KERNEL = 9
GROUPS = 2
SLOT = 512
MIN_LEN = 40
SEQ_DEV = 2
ATT = 384
FFG = 1536
SEQS = 64


def draw_lengths(key, part):
    number_seqs = SEQS
    devices = number_seqs // SEQ_DEV
    key_one, key_two = jax.random.split(key)
    owners = jnp.arange(number_seqs, dtype=jnp.int32) // SEQ_DEV
    ceiling = jax.random.randint(key_one, (devices,), SLOT // 2, SLOT + 1)
    lower = jnp.maximum(MIN_LEN, ceiling // 3)
    picked = jax.random.randint(key_two, (number_seqs,), lower[owners], ceiling[owners] + 1)
    picked = picked.at[0].set(SLOT).at[number_seqs - 1].set(MIN_LEN)
    return picked.astype(jnp.int32)


def strengthened(entries, key, source, target, parts, factor):
    owner, partner = [(jnp.arange(entries.shape[position]) // (entries.shape[position] // parts)).reshape([-1 if axis == position else 1 for axis in range(entries.ndim)]) for position in (source, target)]
    chosen = jax.random.permutation(key, parts)[partner]
    strong = (owner == chosen) | (owner == (partner + parts // 2) % parts)
    return jnp.where(strong, factor * entries, entries)


def shard_levels(stream_key, dims, shards, low, top_value):
    factor_of, own = 1.0, jax.random.fold_in(stream_key, 6)
    for dim, parts in shards:
        draws = jnp.exp(jax.random.uniform(jax.random.fold_in(own, dim), (parts,), jnp.float32, low / len(shards), top_value / len(shards)))
        factor_of = factor_of * jnp.repeat(draws, dims[dim] // parts).reshape([-1 if axis == dim else 1 for axis in range(len(dims))])
    return factor_of


def noise(stream_key, shape, deviation, reach, pieces=(), held_as=jnp.bfloat16):
    level = shard_levels(stream_key, shape, pieces, -0.22, 0.18) if pieces else 1.0
    values = jax.random.normal(stream_key, shape, jnp.float32) * deviation * level
    return jnp.minimum(jnp.maximum(values, -reach), reach).astype(held_as)


def heavy_noise(rng, dims, width, limit, cuts, heavy, held_as=jnp.bfloat16):
    array = width * jax.random.normal(rng, dims, jnp.float32)
    if cuts:
        array = array * shard_levels(rng, dims, cuts, -0.22, 0.18)
    return jnp.clip(strengthened(array, jax.random.fold_in(rng, 3), *heavy), -limit, limit).astype(held_as)


def setup_inputs(seed: int = 0) -> dict:
    key_list = jax.random.split(jax.random.key(seed), 18)
    return {
        "tokens": heavy_noise(key_list[0], (SEQS, SLOT, D), 1.0, 6.0, ((0, 32),), (0, 2, 32, 2.75)),
        "lengths": draw_lengths(jax.random.fold_in(key_list[17], 71), 0),
        "query_weight": noise(key_list[2], (D, ATT), (D // 4) ** -0.5, 0.4375, ((0, 32),)),
        "key_weight": noise(key_list[3], (D, ATT), D ** -0.5, 0.21875, ((0, 32),)),
        "value_weight": noise(key_list[4], (D, ATT), D ** -0.5, 0.21875, ((0, 32),)),
        "depth_weight": noise(key_list[5], (KERNEL, D), KERNEL ** -0.5, 2.0, ((1, 32),)),
        "point_weight": noise(key_list[6], (D, ATT), D ** -0.5, 0.21875, ((0, 32),)),
        "taps_weight": noise(key_list[7], (ATT * HEADS * KERNEL,), ATT ** -0.5, 0.3125, ((0, 32),)),
        "span_weight": noise(key_list[8], (D, ATT), D ** -0.5, 0.21875, ((0, 32),)),
        "output_weight": noise(key_list[9], (D, D), (D // 4) ** -0.5, 0.4375, ((0, 32),)),
        "scaling": jnp.clip(1.0 + 0.1 * jax.random.normal(key_list[10], (D,), jnp.float32), 0.5, 1.5).astype(jnp.bfloat16),
        "offsets": noise(key_list[11], (D,), 0.5, 3.0, ((0, 32),)),
        "inner_weight": noise(key_list[12], (GROUPS, D // GROUPS, FFG), (D // GROUPS) ** -0.5, 0.3125, ((2, 32),)),
        "outer_weight": noise(key_list[13], (GROUPS, FFG, D // GROUPS), FFG ** -0.5, 0.15625, ((1, 32),)),
        "stretch": jnp.clip(1.0 + 0.1 * jax.random.normal(key_list[14], (D,), jnp.float32), 0.5, 1.5).astype(jnp.bfloat16),
        "displace": noise(key_list[15], (D,), 0.5, 3.0, ((0, 32),)),
        "cotangent": noise(key_list[16], (SEQS, SLOT, D), 1.0, 6.0, ((0, 32),)),
    }


@jax.custom_vjp
def low(v):
    return lax.optimization_barrier(v.astype(jnp.bfloat16)).astype(jnp.float32)

@jax.custom_vjp
def low_back(v):
    return v

def low_keep(v):
    return (low(v), None)

def low_pass(kept, grad):
    return (grad,)

def back_keep(v):
    return (v, None)

def back_low(kept, grad):
    return (low(grad),)
low.defvjp(low_keep, low_pass)
low_back.defvjp(back_keep, back_low)
epsilon = 1e-06
masked_score = -1000000000.0
root_half = 0.7071067811865476
highest = lax.Precision.HIGHEST

def rounded(value):
    return low(low_back(value))

def matmul(left, right):
    return jnp.einsum('...k,kn->...n', left, right, precision=highest)

def layer_norm(value, gain, shift):
    mean = lax.optimization_barrier(jnp.mean(value, axis=-1, keepdims=True))
    centered = value - mean
    scale = lax.rsqrt(lax.optimization_barrier(jnp.mean(centered * centered, axis=-1, keepdims=True)) + epsilon)
    return centered * scale * gain + shift

def gelu_exact(value):
    return 0.5 * value * (1.0 + lax.erf(value * root_half))

def shifted_sum(padded, factors, length):
    result = padded[:, 0:length] * factors(0)
    for offset in range(1, KERNEL):
        result = result + padded[:, offset:offset + length] * factors(offset)
    return result

def forward(tokens, valid_rows, weights):
    query_weight, key_weight, value_weight, depth_weight, point_weight, taps_weight, span_weight, output_weight, scaling, offsets, inner_weight, outer_weight, stretch, displace = weights
    seq_count, slot_len = (tokens.shape[0], tokens.shape[1])
    radius = KERNEL // 2
    head_shape = (seq_count, slot_len, HEADS, HEAD)
    masked = tokens * valid_rows[..., None]
    query = rounded(matmul(masked, query_weight))
    keys = rounded(matmul(masked, key_weight))
    values = rounded(matmul(masked, value_weight))
    scores = low_back(jnp.einsum('bshd,bthd->bhst', query.reshape(head_shape), keys.reshape(head_shape), precision=highest) * HEAD ** (-0.5))
    scores = jnp.where(valid_rows[:, None, None, :] > 0, scores, masked_score)
    attention = low(jax.nn.softmax(scores, axis=-1))
    context = rounded(jnp.einsum('bhst,bthd->bshd', attention, values.reshape(head_shape), precision=highest).reshape(seq_count, slot_len, ATT))
    padded = jnp.pad(masked, ((0, 0), (radius, radius), (0, 0)))
    depthwise = low(shifted_sum(padded, lambda offset: depth_weight[offset], slot_len))
    key_conv = low_back(matmul(depthwise, point_weight))
    mixture = low(key_conv * query)
    logits = low_back(matmul(mixture, taps_weight.reshape(ATT, HEADS * KERNEL)))
    tap_weights = jax.nn.softmax(logits.reshape(seq_count, slot_len, HEADS, KERNEL), axis=-1)
    span_values = low_back(matmul(masked, span_weight)).reshape(head_shape)
    span_padded = jnp.pad(span_values, ((0, 0), (radius, radius), (0, 0), (0, 0)))
    span_output = low(shifted_sum(span_padded, lambda offset: tap_weights[..., offset:offset + 1], slot_len).reshape(seq_count, slot_len, ATT))
    joined = jnp.concatenate([context, span_output], axis=-1)
    attended = low_back(matmul(joined, output_weight))
    normed_one = layer_norm(attended + masked, scaling, offsets)
    grouped = (seq_count, slot_len, GROUPS, D // GROUPS)
    hidden = low_back(jnp.einsum('bsgk,gkn->bsgn', low(normed_one).reshape(grouped), inner_weight, precision=highest))
    active = low(gelu_exact(hidden))
    projected = low_back(jnp.einsum('bsgn,gnk->bsgk', active, outer_weight, precision=highest).reshape(seq_count, slot_len, D))
    second = layer_norm(projected + normed_one, stretch, displace)
    return second * valid_rows[..., None]

def reference(tokens, lengths, query_weight, key_weight, value_weight, depth_weight, point_weight, taps_weight, span_weight, output_weight, scaling, offsets, inner_weight, outer_weight, stretch, displace, cotangent):
    weights = tuple((entry.astype(jnp.float32) for entry in (query_weight, key_weight, value_weight, depth_weight, point_weight, taps_weight, span_weight, output_weight, scaling, offsets, inner_weight, outer_weight, stretch, displace)))
    group_size = math.gcd(SEQS, max(1, 4096 // SLOT))
    steps_count = SEQS // group_size
    positions = jnp.arange(SLOT, dtype=jnp.int32)
    valid_rows = (positions[None, :] < lengths[:, None].astype(jnp.int32)).astype(jnp.float32)

    def regroup(values_in):
        return values_in.reshape((steps_count, group_size) + values_in.shape[1:])

    def advance(totals, batch_item):
        token_block, valid_block, cot_block = batch_item
        result, pullback = jax.vjp(lambda inputs, params: forward(inputs, valid_block, params), token_block, weights)
        block_grad, weight_grads = pullback(cot_block)
        totals = jax.tree.map(jnp.add, totals, weight_grads)
        return (totals, (result.astype(jnp.bfloat16), block_grad))
    zero_grads = jax.tree.map(jnp.zeros_like, weights)
    totals, (outputs, input_grads) = lax.scan(advance, zero_grads, (regroup(tokens.astype(jnp.float32)), regroup(valid_rows), regroup(cotangent.astype(jnp.float32))))
    return (outputs.reshape(tokens.shape), input_grads.reshape(tokens.shape).astype(jnp.float32), totals[0], totals[1], totals[2], totals[3], totals[4], totals[5], totals[6], totals[7], totals[8], totals[9], totals[10], totals[11], totals[12], totals[13])
```

```python
import jax
import jax.numpy as jnp
from jax import lax
from jax.sharding import PartitionSpec as P

D = 768
HEADS = 6
HEAD = 64
KERNEL = 9
GROUPS = 2
ATT = 384

epsilon = 1e-06
masked_score = -1000000000.0
root_half = 0.7071067811865476
slope_factor = 0.3989422804014327


def project(left, right):
    return jnp.einsum("bsk,kn->bsn", left, right, preferred_element_type=jnp.float32)


def project_back(grad_out, right):
    return jnp.einsum("bsn,kn->bsk", grad_out, right, preferred_element_type=jnp.float32)


def weight_term(left, grad_out):
    return jnp.einsum("bsk,bsn->kn", left, grad_out, preferred_element_type=jnp.float32)


def norm_forward(value, gain, shift):
    mean = jnp.mean(value, axis=-1, keepdims=True)
    centered = value - mean
    scale = lax.rsqrt(jnp.mean(centered * centered, axis=-1, keepdims=True) + epsilon)
    unit = centered * scale
    return (unit * gain + shift, unit, scale)


def norm_backward(grad_out, unit, scale, gain):
    gain_grad = jnp.sum(grad_out * unit, axis=(0, 1))
    shift_grad = jnp.sum(grad_out, axis=(0, 1))
    scaled = grad_out * gain
    value_grad = scale * (
        scaled
        - jnp.mean(scaled, axis=-1, keepdims=True)
        - unit * jnp.mean(scaled * unit, axis=-1, keepdims=True)
    )
    return (value_grad, gain_grad, shift_grad)


def gelu_exact(value):
    return 0.5 * value * (1.0 + lax.erf(value * root_half))


def gelu_slope(value):
    return (
        0.5 * (1.0 + lax.erf(value * root_half))
        + value * jnp.exp(-0.5 * value * value) * slope_factor
    )


def shifted_sum(padded, factors, length):
    result = padded[:, 0:length] * factors(0)
    for offset in range(1, KERNEL):
        result = result + padded[:, offset : offset + length] * factors(offset)
    return result


def shifted_back(grad_out, factors, radius):
    length = grad_out.shape[1]
    result = None
    for offset in range(2 * radius + 1):
        product = grad_out * factors(offset)
        padding = [(0, 0)] * grad_out.ndim
        padding[1] = (offset, 2 * radius - offset)
        shifted = jnp.pad(product, padding)[:, radius : radius + length]
        result = shifted if result is None else result + shifted
    return result


def masked_scores(query, keys, valid):
    scores = jnp.einsum(
        "shd,thd->hst", query, keys, preferred_element_type=jnp.float32
    ) * query.shape[-1] ** (-0.5)
    return jnp.where(valid[None, None, :] > 0, scores, masked_score)


def attend(entry):
    query, keys, values, valid = entry
    scores = masked_scores(query, keys, valid)
    highest = jnp.max(scores, axis=-1, keepdims=True)
    exponent = jnp.exp(scores - highest)
    totals = jnp.sum(exponent, axis=-1, keepdims=True)
    weights_low = (exponent / totals).astype(jnp.bfloat16)
    context = jnp.einsum("hst,thd->shd", weights_low, values, preferred_element_type=jnp.float32)
    return (context, highest[..., 0] + jnp.log(totals[..., 0]))


def attend_back(entry):
    query, keys, values, valid, logsum, grad_context = entry
    factor = query.shape[-1] ** (-0.5)
    scores = masked_scores(query, keys, valid)
    attention = jnp.exp(scores - logsum[..., None])
    grad_attention = jnp.einsum(
        "shd,thd->hst", grad_context, values, preferred_element_type=jnp.float32
    )
    grad_values = jnp.einsum(
        "hst,shd->thd",
        attention.astype(jnp.bfloat16),
        grad_context,
        preferred_element_type=jnp.float32,
    )
    centre = jnp.sum(attention * grad_attention, axis=-1, keepdims=True)
    grad_scores = (attention * (grad_attention - centre)).astype(jnp.bfloat16)
    grad_query = (
        jnp.einsum("hst,thd->shd", grad_scores, keys, preferred_element_type=jnp.float32) * factor
    )
    grad_keys = (
        jnp.einsum("hst,shd->thd", grad_scores, query, preferred_element_type=jnp.float32) * factor
    )
    return (grad_query, grad_keys, grad_values)


class Links:
    def __init__(self, dp, fsdp):
        self.sizes = {"dp": dp, "fsdp": fsdp}
        outer, inner = [], []
        bit = dp // 2
        while bit >= 1:
            outer.append(("dp", bit))
            bit //= 2
        bit = 2
        while bit < fsdp:
            inner.append(("fsdp", bit))
            bit *= 2
        core = [("fsdp", 1)] if fsdp > 1 else []
        self.orders = (outer + inner + core, outer + inner[::-1] + core)
        bits = dp * fsdp
        self.count = bits
        named = [("dp", 1 << i) for i in range(32) if (1 << i) < dp][::-1]
        named += [("fsdp", 1 << i) for i in range(32) if (1 << i) < fsdp][::-1]
        self.named = named

    def weight(self, stage):
        axis, bit = stage
        return bit * self.sizes["fsdp"] if axis == "dp" else bit

    def swap(self, value, stage):
        axis, bit = stage
        return lax.ppermute(value, axis, [(i, i ^ bit) for i in range(self.sizes[axis])])

    def gather(self, shard, order):
        stages = self.orders[order]
        pieces = [shard[None]]
        for k, stage in enumerate(stages):
            pieces = pieces + [self.swap(p, stage) for p in pieces]
            if k < len(stages) - 3:
                pieces = [jnp.concatenate(pieces, axis=0)]
        return jnp.concatenate(pieces, axis=0)

    def slots_of_owners(self, order):
        stages = self.orders[order]
        me = lax.axis_index("dp") * self.sizes["fsdp"] + lax.axis_index("fsdp")
        rel = jnp.arange(self.count, dtype=jnp.int32) ^ me
        slot = jnp.zeros_like(rel)
        for k, stage in enumerate(stages):
            slot = slot + jnp.where((rel & self.weight(stage)) != 0, 1 << k, 0)
        return slot

    def whole(self, shard, order):
        slots = self.gather(shard, order)
        return jnp.take(slots, self.slots_of_owners(order), axis=0, mode="clip").reshape(-1, shard.shape[-1])

    def reduce_slots(self, slots, order):
        for stage in self.orders[order][::-1]:
            half = slots.shape[0] // 2
            got = self.swap(slots[half:].astype(jnp.bfloat16), stage)
            slots = slots[:half] + got.astype(jnp.float32)
        return slots[0]

    def reduce_owners(self, terms, order):
        cols = terms.shape[-1]
        value = terms.reshape((2,) * len(self.named) + (-1, cols))
        left = list(self.named)
        for stage in self.orders[order][::-1]:
            axis, bit = stage
            dim = left.index(stage)
            mine = (lax.axis_index(axis) // bit) & 1
            send = lax.dynamic_index_in_dim(value, 1 - mine, dim, keepdims=False)
            keep = lax.dynamic_index_in_dim(value, mine, dim, keepdims=False)
            got = self.swap(send.astype(jnp.bfloat16), stage)
            value = keep + got.astype(jnp.float32)
            left.pop(dim)
        return value


def on_device(
    links,
    tokens,
    lengths,
    query_weight,
    key_weight,
    value_weight,
    depth_weight,
    point_weight,
    taps_weight,
    span_weight,
    output_weight,
    scaling,
    offsets,
    inner_weight,
    outer_weight,
    stretch,
    displace,
    cotangent,
):
    rows = query_weight.shape[0]
    low = jnp.bfloat16
    packed = jnp.concatenate(
        [
            depth_weight.T,
            scaling[:, None],
            offsets[:, None],
            stretch[:, None],
            displace[:, None],
            taps_weight.reshape(rows, -1),
        ],
        axis=1,
    )
    used = packed.shape[1]
    packed = jnp.pad(packed, ((0, 0), (0, 128 - used)))
    qk_full = links.whole(jnp.concatenate([query_weight, key_weight], axis=1), 0)
    vs_full = links.whole(jnp.concatenate([value_weight, span_weight], axis=1), 1)
    ps_full = links.whole(jnp.concatenate([point_weight, packed], axis=1), 0)
    output_full = links.whole(output_weight, 1)
    outer_full = [links.gather(outer_weight[g], g).reshape(-1, D // GROUPS) for g in range(GROUPS)]
    inner_full = [links.gather(inner_weight[g].T, g).reshape(-1, D // GROUPS) for g in range(GROUPS)]
    query_full, key_full = qk_full[:, :ATT], qk_full[:, ATT:]
    value_full, span_full = vs_full[:, :ATT], vs_full[:, ATT:]
    point_full, small = ps_full[:, :ATT], ps_full[:, ATT:]
    depth_factors = small[:, :KERNEL].astype(jnp.float32).T
    scaling_full, offsets_full, stretch_full, displace_full = (
        small[:, KERNEL + i].astype(jnp.float32) for i in range(4)
    )
    taps_full = small[:, KERNEL + 4 : used].reshape(ATT, HEADS * KERNEL)

    seq_count, slot_len = (tokens.shape[0], tokens.shape[1])
    radius = KERNEL // 2
    head_shape = (seq_count, slot_len, HEADS, HEAD)
    positions = lax.broadcasted_iota(jnp.int32, (seq_count, slot_len), 1)
    valid_rows = (positions < lengths[:, None]).astype(jnp.float32)
    masked = tokens * valid_rows[..., None].astype(low)
    query = project(masked, query_full).astype(low)
    keys = project(masked, key_full).astype(low)
    values = project(masked, value_full).astype(low)
    query_heads = query.reshape(head_shape)
    keys_heads = keys.reshape(head_shape)
    values_heads = values.reshape(head_shape)
    context, logsum = lax.map(attend, (query_heads, keys_heads, values_heads, valid_rows))
    context = context.reshape(seq_count, slot_len, ATT).astype(low)
    padded = jnp.pad(masked, ((0, 0), (radius, radius), (0, 0)))
    depthwise = shifted_sum(padded, lambda offset: depth_factors[offset], slot_len).astype(low)
    key_conv = project(depthwise, point_full)
    mixture = (key_conv * query).astype(low)
    logits = project(mixture, taps_full).reshape(seq_count, slot_len, HEADS, KERNEL)
    tap_weights = jax.nn.softmax(logits, axis=-1)
    span_values = project(masked, span_full).reshape(head_shape)
    span_padded = jnp.pad(span_values, ((0, 0), (radius, radius), (0, 0), (0, 0)))
    span_output = (
        shifted_sum(span_padded, lambda offset: tap_weights[..., offset : offset + 1], slot_len)
        .reshape(seq_count, slot_len, ATT)
        .astype(low)
    )
    joined = jnp.concatenate([context, span_output], axis=-1)
    attended = project(joined, output_full)
    normed_one, unit_one, scale_one = norm_forward(attended + masked, scaling_full, offsets_full)
    wide = D // GROUPS
    normed_low = normed_one.astype(low)
    normed_groups = [normed_low[..., g * wide : (g + 1) * wide] for g in range(GROUPS)]
    hidden = [project_back(normed_groups[g], inner_full[g]) for g in range(GROUPS)]
    active = [gelu_exact(h).astype(low) for h in hidden]
    projected = jnp.concatenate([project(active[g], outer_full[g]) for g in range(GROUPS)], axis=-1)
    second, unit_two, scale_two = norm_forward(projected + normed_one, stretch_full, displace_full)
    activations = (second * valid_rows[..., None]).astype(low)

    grad_second = cotangent.astype(jnp.float32) * valid_rows[..., None]
    grad_sum_two, stretch_grad, displace_grad = norm_backward(
        grad_second, unit_two, scale_two, stretch_full
    )
    grad_projected = grad_sum_two.astype(low)
    grad_groups = [grad_projected[..., g * wide : (g + 1) * wide] for g in range(GROUPS)]
    outer_terms, inner_terms, grad_parts = [], [], []
    for g in range(GROUPS):
        outer_terms.append(weight_term(active[g], grad_groups[g]))
        grad_active = project_back(grad_groups[g], outer_full[g])
        grad_hidden = (grad_active * gelu_slope(hidden[g])).astype(low)
        inner_terms.append(weight_term(grad_hidden, normed_groups[g]))
        grad_parts.append(project(grad_hidden, inner_full[g]))
    outer_sum = [
        links.reduce_slots(outer_terms[g].reshape(links.count, -1, wide), g) for g in range(GROUPS)
    ]
    inner_sum = [
        links.reduce_slots(inner_terms[g].reshape(links.count, -1, wide), g) for g in range(GROUPS)
    ]
    grad_normed = grad_sum_two + jnp.concatenate(grad_parts, axis=-1)
    grad_sum_one, scaling_grad, offsets_grad = norm_backward(
        grad_normed, unit_one, scale_one, scaling_full
    )
    grad_attended = grad_sum_one.astype(low)
    output_sum = links.reduce_owners(weight_term(joined, grad_attended), 0)
    grad_joined = project_back(grad_attended, output_full)
    grad_context = grad_joined[..., :ATT].astype(low).reshape(head_shape)
    grad_span = grad_joined[..., ATT:].reshape(head_shape)
    grad_taps = jnp.stack(
        [
            jnp.sum(grad_span * span_padded[:, offset : offset + slot_len], axis=-1)
            for offset in range(KERNEL)
        ],
        axis=-1,
    )
    grad_span_values = (
        shifted_back(grad_span, lambda offset: tap_weights[..., offset : offset + 1], radius)
        .reshape(seq_count, slot_len, ATT)
        .astype(low)
    )
    grad_logits = tap_weights * (
        grad_taps - jnp.sum(tap_weights * grad_taps, axis=-1, keepdims=True)
    )
    grad_logits = grad_logits.reshape(seq_count, slot_len, HEADS * KERNEL).astype(low)
    taps_grad = weight_term(mixture, grad_logits)
    grad_mixture = project_back(grad_logits, taps_full)
    grad_key_conv = (grad_mixture * query).astype(low)
    point_grad = weight_term(depthwise, grad_key_conv)
    grad_depthwise = project_back(grad_key_conv, point_full)
    depth_grad = jnp.stack(
        [
            jnp.sum(grad_depthwise * padded[:, offset : offset + slot_len], axis=(0, 1))
            for offset in range(KERNEL)
        ],
        axis=0,
    )
    small_terms = jnp.concatenate(
        [
            depth_grad.T,
            scaling_grad[:, None],
            offsets_grad[:, None],
            stretch_grad[:, None],
            displace_grad[:, None],
            taps_grad.reshape(D, -1),
        ],
        axis=1,
    )
    small_terms = jnp.pad(small_terms, ((0, 0), (0, 128 - used)))
    ps_sum = links.reduce_owners(jnp.concatenate([point_grad, small_terms], axis=1), 1)
    grad_query_att, grad_keys, grad_values = lax.map(
        attend_back, (query_heads, keys_heads, values_heads, valid_rows, logsum, grad_context)
    )
    grad_query = (
        grad_query_att.reshape(seq_count, slot_len, ATT) + grad_mixture * key_conv
    ).astype(low)
    grad_keys = grad_keys.reshape(seq_count, slot_len, ATT).astype(low)
    grad_values = grad_values.reshape(seq_count, slot_len, ATT).astype(low)
    qk_sum = links.reduce_owners(
        weight_term(masked, jnp.concatenate([grad_query, grad_keys], axis=-1)), 0
    )
    vs_sum = links.reduce_owners(
        weight_term(masked, jnp.concatenate([grad_values, grad_span_values], axis=-1)), 1
    )
    grad_masked = (
        grad_sum_one
        + project_back(grad_query, query_full)
        + project_back(grad_keys, key_full)
        + project_back(grad_values, value_full)
        + project_back(grad_span_values, span_full)
        + shifted_back(grad_depthwise, lambda offset: depth_factors[offset], radius)
    )
    tokens_grad = grad_masked * valid_rows[..., None]
    small_sum = ps_sum[:, ATT:]
    return (
        activations,
        tokens_grad,
        qk_sum[:, :ATT],
        qk_sum[:, ATT:],
        vs_sum[:, :ATT],
        small_sum[:, :KERNEL].T,
        ps_sum[:, :ATT],
        small_sum[:, KERNEL + 4 : used].reshape(-1),
        vs_sum[:, ATT:],
        output_sum,
        small_sum[:, KERNEL],
        small_sum[:, KERNEL + 1],
        jnp.stack([s.T for s in inner_sum]),
        jnp.stack(outer_sum),
        small_sum[:, KERNEL + 2],
        small_sum[:, KERNEL + 3],
    )


def solution(mesh):
    both = ("dp", "fsdp")
    weights = (
        P(both, None),
        P(both, None),
        P(both, None),
        P(None, both),
        P(both, None),
        P(both),
        P(both, None),
        P(both, None),
        P(both),
        P(both),
        P(None, None, both),
        P(None, both, None),
        P(both),
        P(both),
    )
    row = P(both, None, None)
    links = Links(mesh.shape["dp"], mesh.shape["fsdp"])

    def body(*args):
        return on_device(links, *args)

    return jax.shard_map(
        body,
        mesh=mesh,
        in_specs=(row, P(both)) + weights + (row,),
        out_specs=(row, row) + weights,
        check_vma=False,
    )
```

```python
import jax
import jax.numpy as jnp
from jax import lax
from jax.experimental import pallas as pl
from jax.experimental.pallas import tpu as pltpu
from jax.sharding import PartitionSpec as P

D = 768
HEADS = 6
HEAD = 64
KERNEL = 9
GROUPS = 2
ATT = 384

epsilon = 1e-06
masked_score = -1000000000.0
root_half = 0.7071067811865476
slope_factor = 0.3989422804014327


def project(left, right):
    return jnp.einsum("bsk,kn->bsn", left, right, preferred_element_type=jnp.float32)


def project_back(grad_out, right):
    return jnp.einsum("bsn,kn->bsk", grad_out, right, preferred_element_type=jnp.float32)


def weight_term(left, grad_out):
    return jnp.einsum("bsk,bsn->kn", left, grad_out, preferred_element_type=jnp.float32)


def norm_forward(value, gain, shift):
    mean = jnp.mean(value, axis=-1, keepdims=True)
    centered = value - mean
    scale = lax.rsqrt(jnp.mean(centered * centered, axis=-1, keepdims=True) + epsilon)
    unit = centered * scale
    return (unit * gain + shift, unit, scale)


def norm_backward(grad_out, unit, scale, gain):
    gain_grad = jnp.sum(grad_out * unit, axis=(0, 1))
    shift_grad = jnp.sum(grad_out, axis=(0, 1))
    scaled = grad_out * gain
    value_grad = scale * (
        scaled
        - jnp.mean(scaled, axis=-1, keepdims=True)
        - unit * jnp.mean(scaled * unit, axis=-1, keepdims=True)
    )
    return (value_grad, gain_grad, shift_grad)


def gelu_exact(value):
    return 0.5 * value * (1.0 + lax.erf(value * root_half))


def gelu_slope(value):
    return (
        0.5 * (1.0 + lax.erf(value * root_half))
        + value * jnp.exp(-0.5 * value * value) * slope_factor
    )


CHUNK = 128
HALO = 8
SLOTS = 8
WIDE = D // GROUPS


def dot(a, b):
    return jnp.dot(a, b, preferred_element_type=jnp.float32)


def dot_nt(a, b):
    return lax.dot_general(a, b, (((1,), (1,)), ((), ())), preferred_element_type=jnp.float32)


def dot_tn(a, b):
    return lax.dot_general(a, b, (((0,), (0,)), ((), ())), preferred_element_type=jnp.float32)


def lane_of(shape):
    return lax.broadcasted_iota(jnp.int32, shape, len(shape) - 1)


def row_of(shape):
    return lax.broadcasted_iota(jnp.int32, shape, len(shape) - 2)


def shifted(value, offset, count):
    if offset % 8:
        value = pltpu.roll(value, value.shape[0] - offset, axis=0)
        offset = 0
    return value[offset : offset + count]


def high_low(value):
    high = value.astype(jnp.bfloat16)
    low = (value - high.astype(jnp.float32)).astype(jnp.bfloat16)
    return jnp.concatenate([high, low], axis=1)


def over_taps(value, combine):
    for step in (8, 16, 32, 64):
        value = combine(value, pltpu.roll(value, step, axis=1))
    return value


def fill_spread(spread_ref):
    shape = (256, ATT)
    for m in range(KERNEL):
        lanes = row_of(shape) % 128
        head = lane_of(shape) // HEAD
        spread_ref[m] = jnp.where(lanes == m * SLOTS + head, 1.0, 0.0).astype(jnp.bfloat16)


def pad_rows(ref, length):
    zeros = jnp.zeros((HALO, ref.shape[1]), ref.dtype)
    ref[0:HALO, :] = zeros
    ref[HALO + length : 2 * HALO + length, :] = zeros


def forward_kernel(
    lengths_ref, tokens_ref, first_ref, second_ref, taps_ref, depth_ref,
    query_ref, keys_ref, values_ref, conv_ref, depthwise_ref, mixture_ref, tapw_ref, span_ref,
    joined_ref, logsum_ref, padded_ref, span_padded_ref, spread_ref,
):
    length = tokens_ref.shape[1]
    count = lengths_ref[pl.program_id(0)]
    low = jnp.bfloat16

    @pl.when(pl.program_id(0) == 0)
    def _():
        fill_spread(spread_ref)

    pad_rows(padded_ref, length)
    pad_rows(span_padded_ref, length)
    tokens = tokens_ref[0]
    masked = jnp.where(row_of(tokens.shape) < count, tokens.astype(jnp.float32), 0.0)
    padded_ref[HALO : HALO + length, :] = masked
    masked = masked.astype(low)
    query_ref[0] = dot(masked, first_ref[:, :ATT]).astype(low)
    keys_ref[0] = dot(masked, first_ref[:, ATT : 2 * ATT]).astype(low)
    values_ref[0] = dot(masked, second_ref[:, :ATT]).astype(low)
    span = dot(masked, second_ref[:, ATT : 2 * ATT])
    span_ref[0] = span
    span_padded_ref[HALO : HALO + length, :] = span

    def depth_chunk(i, carry):
        start = pl.multiple_of(i * CHUNK, CHUNK)
        block = padded_ref[pl.ds(start, CHUNK + 2 * HALO), :]
        total = None
        for m in range(KERNEL):
            term = shifted(block, HALO - KERNEL // 2 + m, CHUNK) * depth_ref[m : m + 1, :]
            total = term if total is None else total + term
        depthwise_ref[0, pl.ds(start, CHUNK), :] = total.astype(low)
        return carry

    lax.fori_loop(0, length // CHUNK, depth_chunk, 0)
    conv = dot(depthwise_ref[0], first_ref[:, 2 * ATT : 3 * ATT])
    conv_ref[0] = conv
    mixture_ref[0] = (conv * query_ref[0].astype(jnp.float32)).astype(low)
    logits = dot(mixture_ref[0], taps_ref[...])
    logits = jnp.where(lane_of(logits.shape) < KERNEL * SLOTS, logits, -1e30)
    exponent = jnp.exp(logits - over_taps(logits, jnp.maximum))
    tapw_ref[0] = exponent / over_taps(exponent, jnp.add)

    def span_chunk(i, carry):
        start = pl.multiple_of(i * CHUNK, CHUNK)
        block = span_padded_ref[pl.ds(start, CHUNK + 2 * HALO), :]
        both = high_low(tapw_ref[0, pl.ds(start, CHUNK), :])
        total = None
        for m in range(KERNEL):
            term = shifted(block, HALO - KERNEL // 2 + m, CHUNK) * dot(both, spread_ref[m])
            total = term if total is None else total + term
        joined_ref[0, pl.ds(start, CHUNK), ATT:] = total.astype(low)
        return carry

    lax.fori_loop(0, length // CHUNK, span_chunk, 0)

    rows = 256

    def attend_pair(index, carry):
        pair, half = index // (length // rows), index % (length // rows)
        lanes = pl.ds(pl.multiple_of(pair * 128, 128), 128)
        place = pl.ds(pl.multiple_of(half * rows, rows), rows)
        query = query_ref[0, place, lanes]
        keys = keys_ref[0, :, lanes]
        values = values_ref[0, :, lanes]
        left = lane_of((rows, 128)) < HEAD
        sums = logsum_ref[0, place, :]
        contexts = []
        for j in range(2):
            mine = left if j == 0 else jnp.logical_not(left)
            own = jnp.where(mine, query.astype(jnp.float32), 0.0).astype(low)
            scores = dot_nt(own, keys) * HEAD ** (-0.5)
            scores = jnp.where(lane_of(scores.shape) < count, scores, masked_score)
            highest = jnp.max(scores, axis=-1, keepdims=True)
            exponent = jnp.exp(scores - highest)
            totals = jnp.sum(exponent, axis=-1, keepdims=True)
            contexts.append(dot((exponent * (1.0 / totals)).astype(low), values))
            sums = jnp.where(lane_of(sums.shape) == pair * 2 + j, highest + jnp.log(totals), sums)
        logsum_ref[0, place, :] = sums
        joined_ref[0, place, lanes] = jnp.where(left, contexts[0], contexts[1]).astype(low)
        return carry

    logsum_ref[0] = jnp.zeros(logsum_ref.shape[1:], jnp.float32)
    lax.fori_loop(0, (HEADS // 2) * (length // rows), attend_pair, 0)


def whole_spec(shape):
    return pl.BlockSpec(shape, lambda i, *_: (0,) * len(shape))


def seq_spec(length, width):
    return pl.BlockSpec((1, length, width), lambda i, *_: (i, 0, 0))


LIMIT = pltpu.CompilerParams(vmem_limit_bytes=60 * 1024 * 1024, dimension_semantics=("arbitrary",))


def forward_call(lengths, tokens, first, second, taps, depth):
    seqs, length, _ = tokens.shape
    low, full = jnp.bfloat16, jnp.float32
    outs = [
        (ATT, low), (ATT, low), (ATT, low), (ATT, full), (D, low), (ATT, low), (128, full),
        (ATT, full), (D, low), (128, full),
    ]
    return pl.pallas_call(
        forward_kernel,
        grid_spec=pltpu.PrefetchScalarGridSpec(
            num_scalar_prefetch=1,
            grid=(seqs,),
            in_specs=[seq_spec(length, D)]
            + [whole_spec(a.shape) for a in (first, second, taps, depth)],
            out_specs=[seq_spec(length, w) for w, _ in outs],
            scratch_shapes=[
                pltpu.VMEM((length + 2 * HALO, D), full),
                pltpu.VMEM((length + 2 * HALO, ATT), full),
                pltpu.VMEM((KERNEL, 256, ATT), low),
            ],
        ),
        out_shape=[jax.ShapeDtypeStruct((seqs, length, w), t) for w, t in outs],
        compiler_params=LIMIT,
        name="layer_forward",
    )(lengths, tokens, first, second, taps, depth)


def conv_back_kernel(
    lengths_ref, tokens_ref, grad_span_ref, tapw_ref, span_ref, mixture_ref, query_ref, conv_ref,
    depthwise_ref, point_ref, taps_ref, depth_ref,
    grad_spanv_ref, grad_mixconv_ref, grad_tokens_ref, taps_grad_ref, point_grad_ref,
    depth_grad_ref,
    padded_ref, span_padded_ref, grad_padded_ref, tapw_padded_ref, back_padded_ref, logit_ref,
    sums_ref, spread_ref, gather_ref,
):
    length = tokens_ref.shape[1]
    count = lengths_ref[pl.program_id(0)]
    low = jnp.bfloat16
    begin = pl.program_id(0) == 0

    @pl.when(begin)
    def _():
        fill_spread(spread_ref)
        shape = (ATT, 128)
        for m in range(KERNEL):
            hit = lane_of(shape) == m * SLOTS + row_of(shape) // HEAD
            gather_ref[m] = jnp.where(hit, 1.0, 0.0).astype(low)
        taps_grad_ref[...] = jnp.zeros(taps_grad_ref.shape, jnp.float32)
        point_grad_ref[...] = jnp.zeros(point_grad_ref.shape, jnp.float32)
        sums_ref[...] = jnp.zeros(sums_ref.shape, jnp.float32)

    inside = slice(HALO, HALO + length)
    for ref in (padded_ref, span_padded_ref, grad_padded_ref, tapw_padded_ref, back_padded_ref):
        pad_rows(ref, length)
    tokens = tokens_ref[0]
    padded_ref[inside, :] = jnp.where(row_of(tokens.shape) < count, tokens.astype(jnp.float32), 0.0)
    span_padded_ref[inside, :] = span_ref[0]
    grad_padded_ref[inside, :] = grad_span_ref[0]
    tapw_padded_ref[inside, :] = tapw_ref[0]

    def span_chunk(i, carry):
        start = pl.multiple_of(i * CHUNK, CHUNK)
        place = pl.ds(start, CHUNK)
        around = pl.ds(start, CHUNK + 2 * HALO)
        spans = span_padded_ref[around, :]
        grads = grad_padded_ref[around, :]
        both = high_low(tapw_padded_ref[around, :])
        own = grads[HALO : HALO + CHUNK]
        grad_taps = None
        total = None
        for m in range(KERNEL):
            product = shifted(spans, HALO - KERNEL // 2 + m, CHUNK) * own
            part = dot(product.astype(low), gather_ref[m])
            grad_taps = part if grad_taps is None else grad_taps + part
            spread = dot(both, spread_ref[m]) * grads
            term = shifted(spread, HALO + KERNEL // 2 - m, CHUNK)
            total = term if total is None else total + term
        grad_spanv_ref[0, place, :] = total.astype(low)
        weights = tapw_ref[0, place, :]
        centre = over_taps(weights * grad_taps, jnp.add)
        logit_ref[place, :] = (weights * (grad_taps - centre)).astype(low)
        return carry

    lax.fori_loop(0, length // CHUNK, span_chunk, 0)
    grad_logits = logit_ref[...]
    taps_grad_ref[...] += dot_tn(mixture_ref[0], grad_logits)
    grad_mixture = dot_nt(grad_logits, taps_ref[...])
    grad_conv = (grad_mixture * query_ref[0].astype(jnp.float32)).astype(low)
    grad_mixconv_ref[0] = grad_mixture * conv_ref[0]
    point_grad_ref[...] += dot_tn(depthwise_ref[0], grad_conv)
    back_padded_ref[inside, :] = dot_nt(grad_conv, point_ref[...])

    def depth_chunk(i, carry):
        start = pl.multiple_of(i * CHUNK, CHUNK)
        around = pl.ds(start, CHUNK + 2 * HALO)
        tokens = padded_ref[around, :]
        grads = back_padded_ref[around, :]
        own = grads[HALO : HALO + CHUNK]
        total = None
        for m in range(KERNEL):
            product = shifted(tokens, HALO - KERNEL // 2 + m, CHUNK) * own
            part = product[0:8]
            for r in range(8, CHUNK, 8):
                part = part + product[r : r + 8]
            sums_ref[m * 8 : m * 8 + 8, :] += part
            term = shifted(grads, HALO + KERNEL // 2 - m, CHUNK) * depth_ref[m : m + 1, :]
            total = term if total is None else total + term
        grad_tokens_ref[0, pl.ds(start, CHUNK), :] = total
        return carry

    lax.fori_loop(0, length // CHUNK, depth_chunk, 0)

    @pl.when(pl.program_id(0) == pl.num_programs(0) - 1)
    def _():
        for m in range(KERNEL):
            depth_grad_ref[m : m + 1, :] = jnp.sum(
                sums_ref[m * 8 : m * 8 + 8, :], axis=0, keepdims=True
            )
        depth_grad_ref[KERNEL:16, :] = jnp.zeros((16 - KERNEL, D), jnp.float32)


def conv_back_call(
    lengths, tokens, grad_span, tapw, span, mixture, query, conv, depthwise, point, taps, depth
):
    seqs, length, _ = tokens.shape
    low, full = jnp.bfloat16, jnp.float32
    rows = length + 2 * HALO
    return pl.pallas_call(
        conv_back_kernel,
        grid_spec=pltpu.PrefetchScalarGridSpec(
            num_scalar_prefetch=1,
            grid=(seqs,),
            in_specs=[
                seq_spec(length, a.shape[2])
                for a in (tokens, grad_span, tapw, span, mixture, query, conv, depthwise)
            ]
            + [whole_spec(a.shape) for a in (point, taps, depth)],
            out_specs=[seq_spec(length, w) for w in (ATT, ATT, D)]
            + [whole_spec(s) for s in ((ATT, 128), (D, ATT), (16, D))],
            scratch_shapes=[
                pltpu.VMEM((rows, D), full),
                pltpu.VMEM((rows, ATT), full),
                pltpu.VMEM((rows, ATT), full),
                pltpu.VMEM((rows, 128), full),
                pltpu.VMEM((rows, D), full),
                pltpu.VMEM((length, 128), low),
                pltpu.VMEM((KERNEL * 8, D), full),
                pltpu.VMEM((KERNEL, 256, ATT), low),
                pltpu.VMEM((KERNEL, ATT, 128), low),
            ],
        ),
        out_shape=[
            jax.ShapeDtypeStruct((seqs, length, ATT), low),
            jax.ShapeDtypeStruct((seqs, length, ATT), full),
            jax.ShapeDtypeStruct((seqs, length, D), full),
            jax.ShapeDtypeStruct((ATT, 128), full),
            jax.ShapeDtypeStruct((D, ATT), full),
            jax.ShapeDtypeStruct((16, D), full),
        ],
        compiler_params=LIMIT,
        name="conv_back",
    )(lengths, tokens, grad_span, tapw, span, mixture, query, conv, depthwise, point, taps, depth)


def attend_back_kernel(
    lengths_ref, query_ref, keys_ref, values_ref, logsum_ref, grad_context_ref, mixconv_ref,
    grad_query_ref, grad_keys_ref, grad_values_ref,
    turned_ref, keys_sum_ref, values_sum_ref,
):
    length = query_ref.shape[1]
    count = lengths_ref[pl.program_id(0)]
    low = jnp.bfloat16
    factor = HEAD ** (-0.5)
    turned_ref[...] = logsum_ref[0].T
    keys_sum_ref[...] = jnp.zeros(keys_sum_ref.shape, jnp.float32)
    values_sum_ref[...] = jnp.zeros(values_sum_ref.shape, jnp.float32)
    part = 256

    for pair in range(HEADS // 2):
        lanes = slice(pair * 128, pair * 128 + 128)

        def chunk(i, carry, pair=pair, lanes=lanes):
            place = pl.ds(pl.multiple_of(i * part, part), part)
            keys = keys_ref[0, :, lanes]
            values = values_ref[0, :, lanes]
            query = query_ref[0, place, lanes].astype(jnp.float32)
            grads = grad_context_ref[0, place, lanes].astype(jnp.float32)
            total = mixconv_ref[0, place, lanes]
            for j in range(2):
                own = lane_of((part, 128)) // HEAD == j
                query_j = jnp.where(own, query, 0.0).astype(low)
                grads_j = jnp.where(own, grads, 0.0).astype(low)
                scores = dot_nt(keys, query_j) * factor
                attention = jnp.exp(scores - turned_ref[pair * 2 + j : pair * 2 + j + 1, place])
                attention = jnp.where(row_of(scores.shape) < count, attention, 0.0)
                grad_attention = dot_nt(values, grads_j)
                values_sum_ref[:, lanes] += dot(attention.astype(low), grads_j)
                centre = jnp.sum(attention * grad_attention, axis=0, keepdims=True)
                grad_scores = (attention * (grad_attention - centre)).astype(low)
                keys_sum_ref[:, lanes] += dot(grad_scores, query_j)
                both = dot_tn(grad_scores, keys)
                total = total + jnp.where(own, both, 0.0) * factor
            grad_query_ref[0, place, lanes] = total.astype(low)
            return carry

        lax.fori_loop(0, length // part, chunk, 0)
    grad_keys_ref[0] = (keys_sum_ref[...] * factor).astype(low)
    grad_values_ref[0] = values_sum_ref[...].astype(low)


def attend_back_call(lengths, query, keys, values, logsum, grad_context, mixconv):
    seqs, length, _ = query.shape
    low, full = jnp.bfloat16, jnp.float32
    return pl.pallas_call(
        attend_back_kernel,
        grid_spec=pltpu.PrefetchScalarGridSpec(
            num_scalar_prefetch=1,
            grid=(seqs,),
            in_specs=[
                seq_spec(length, a.shape[2])
                for a in (query, keys, values, logsum, grad_context, mixconv)
            ],
            out_specs=[seq_spec(length, ATT)] * 3,
            scratch_shapes=[
                pltpu.VMEM((128, length), full),
                pltpu.VMEM((length, ATT), full),
                pltpu.VMEM((length, ATT), full),
            ],
        ),
        out_shape=[jax.ShapeDtypeStruct((seqs, length, ATT), low)] * 3,
        compiler_params=LIMIT,
        name="attend_back",
    )(lengths, query, keys, values, logsum, grad_context, mixconv)


class Links:
    def __init__(self, dp, fsdp):
        self.sizes = {"dp": dp, "fsdp": fsdp}
        self.outer = [("dp", 1 << i) for i in range(32) if (1 << i) < dp][::-1]
        inner = [("fsdp", 1 << i) for i in range(1, 32) if (1 << i) < fsdp]
        core = [("fsdp", 1)] if fsdp > 1 else []
        self.tails = (inner + core, inner[::-1] + core)
        self.count = dp * fsdp
        self.named = self.outer + [("fsdp", 1 << i) for i in range(32) if (1 << i) < fsdp][::-1]

    def weight(self, stage):
        axis, bit = stage
        return bit * self.sizes["fsdp"] if axis == "dp" else bit

    def swap(self, value, stage):
        axis, bit = stage
        return lax.ppermute(value, axis, [(i, i ^ bit) for i in range(self.sizes[axis])])

    def grow(self, blocks, stages):
        for stage in stages:
            blocks = jnp.concatenate([blocks, self.swap(blocks, stage)], axis=0)
        return blocks

    def gather(self, shard, order):
        return self.grow(self.grow(shard[None], self.outer), self.tails[order])

    def gather_two(self, first, second):
        cut = first.shape[1]
        blocks = self.grow(jnp.concatenate([first, second], axis=1)[None], self.outer)
        parts = (blocks[..., :cut], blocks[..., cut:])
        return tuple(
            jnp.take(
                self.grow(parts[i], self.tails[i]), self.slots_of_owners(i), axis=0, mode="clip"
            ).reshape(-1, parts[i].shape[-1])
            for i in range(2)
        )

    def slots_of_owners(self, order):
        me = lax.axis_index("dp") * self.sizes["fsdp"] + lax.axis_index("fsdp")
        rel = jnp.arange(self.count, dtype=jnp.int32) ^ me
        slot = jnp.zeros_like(rel)
        for k, stage in enumerate(self.outer + self.tails[order]):
            slot = slot + jnp.where((rel & self.weight(stage)) != 0, 1 << k, 0)
        return slot

    def reduce_slots(self, terms, order):
        for stage in (self.outer + self.tails[order])[::-1]:
            half = terms[0].shape[0] // 2
            send = jnp.concatenate([t[half:].astype(jnp.bfloat16) for t in terms], axis=1)
            got = self.swap(send, stage)
            keep = jnp.concatenate([t[:half] for t in terms], axis=1)
            terms = [(yield keep + got.astype(jnp.float32))]

    def shrink(self, terms, left, stages):
        left = list(left)
        for stage in stages:
            axis, bit = stage
            dim = left.index(stage)
            mine = (lax.axis_index(axis) // bit) & 1
            send = [
                lax.dynamic_index_in_dim(t, 1 - mine, dim, keepdims=False).astype(jnp.bfloat16)
                for t in terms
            ]
            keep = [lax.dynamic_index_in_dim(t, mine, dim, keepdims=False) for t in terms]
            got = self.swap(jnp.concatenate(send, axis=-1), stage)
            terms = [jnp.concatenate(keep, axis=-1) + got.astype(jnp.float32)]
            left.pop(dim)
        return terms, left

    def reduce_two(self, first, second):
        sums = []
        for i, terms in enumerate((first, second)):
            split = [t.reshape((2,) * len(self.named) + (-1, t.shape[-1])) for t in terms]
            done, left = self.shrink(split, self.named, self.tails[i][::-1])
            sums += done
        both, _ = self.shrink(sums, left, self.outer[::-1])
        return both[0]


def on_device(
    links,
    tokens,
    lengths,
    query_weight,
    key_weight,
    value_weight,
    depth_weight,
    point_weight,
    taps_weight,
    span_weight,
    output_weight,
    scaling,
    offsets,
    inner_weight,
    outer_weight,
    stretch,
    displace,
    cotangent,
):
    rows = query_weight.shape[0]
    low = jnp.bfloat16
    packed = jnp.concatenate(
        [
            depth_weight.T,
            scaling[:, None],
            offsets[:, None],
            stretch[:, None],
            displace[:, None],
            taps_weight.reshape(rows, -1),
        ],
        axis=1,
    )
    used = packed.shape[1]
    packed = jnp.pad(packed, ((0, 0), (0, 128 - used)))
    first, second = links.gather_two(
        jnp.concatenate([query_weight, key_weight, point_weight, packed], axis=1),
        jnp.concatenate([value_weight, span_weight, output_weight], axis=1),
    )
    query_full, key_full, point_full, small = (
        first[:, :ATT],
        first[:, ATT : 2 * ATT],
        first[:, 2 * ATT : 3 * ATT],
        first[:, 3 * ATT :],
    )
    value_full, span_full, output_full = (
        second[:, :ATT],
        second[:, ATT : 2 * ATT],
        second[:, 2 * ATT :],
    )
    wide = D // GROUPS
    grouped_shard = jnp.concatenate(
        [outer_weight[0], outer_weight[1], inner_weight[0].T, inner_weight[1].T], axis=1
    )
    grouped_full = links.gather(grouped_shard, 0).reshape(-1, 2 * D)
    outer_full = [grouped_full[:, g * wide : (g + 1) * wide] for g in range(GROUPS)]
    inner_full = [grouped_full[:, D + g * wide : D + (g + 1) * wide] for g in range(GROUPS)]
    depth_full = small[:, :KERNEL].astype(jnp.float32).T
    depth_full = jnp.pad(depth_full, ((0, 16 - KERNEL), (0, 0)))
    scaling_full, offsets_full, stretch_full, displace_full = (
        small[:, KERNEL + i].astype(jnp.float32) for i in range(4)
    )
    taps_full = small[:, KERNEL + 4 : used].reshape(ATT, HEADS, KERNEL).swapaxes(1, 2)
    taps_full = jnp.pad(taps_full, ((0, 0), (0, 0), (0, SLOTS - HEADS))).reshape(ATT, -1)
    taps_full = jnp.pad(taps_full, ((0, 0), (0, 128 - KERNEL * SLOTS)))

    seq_count, slot_len = (tokens.shape[0], tokens.shape[1])
    positions = lax.broadcasted_iota(jnp.int32, (seq_count, slot_len), 1)
    valid_rows = (positions < lengths[:, None]).astype(jnp.float32)
    masked = tokens * valid_rows[..., None].astype(low)
    (
        query, keys, values, key_conv, depthwise, mixture, tap_weights, span_values, joined, logsum,
    ) = forward_call(lengths, tokens, first, second, taps_full, depth_full)
    attended = project(joined, output_full)
    normed_one, unit_one, scale_one = norm_forward(attended + masked, scaling_full, offsets_full)
    normed_low = normed_one.astype(low)
    normed_groups = [normed_low[..., g * wide : (g + 1) * wide] for g in range(GROUPS)]
    hidden = [project_back(normed_groups[g], inner_full[g]) for g in range(GROUPS)]
    active = [gelu_exact(h).astype(low) for h in hidden]
    projected = jnp.concatenate([project(active[g], outer_full[g]) for g in range(GROUPS)], axis=-1)
    second, unit_two, scale_two = norm_forward(projected + normed_one, stretch_full, displace_full)
    activations = (second * valid_rows[..., None]).astype(low)

    grad_second = cotangent.astype(jnp.float32) * valid_rows[..., None]
    grad_sum_two, stretch_grad, displace_grad = norm_backward(
        grad_second, unit_two, scale_two, stretch_full
    )
    grad_projected = grad_sum_two.astype(low)
    grad_groups = [grad_projected[..., g * wide : (g + 1) * wide] for g in range(GROUPS)]
    outer_terms, inner_terms, grad_parts = [], [], []
    for g in range(GROUPS):
        outer_terms.append(weight_term(active[g], grad_groups[g]))
        grad_active = project_back(grad_groups[g], outer_full[g])
        grad_hidden = (grad_active * gelu_slope(hidden[g])).astype(low)
        inner_terms.append(weight_term(grad_hidden, normed_groups[g]))
        grad_parts.append(project(grad_hidden, inner_full[g]))
    reduction = links.reduce_slots(outer_terms + inner_terms, 0)
    grouped_sum = next(reduction)
    ended = False

    def behind(value):
        nonlocal grouped_sum, ended
        if ended:
            return value
        value, grouped_sum = lax.optimization_barrier((value, grouped_sum))
        try:
            grouped_sum = reduction.send(grouped_sum)
        except StopIteration:
            ended = True
        return value

    grad_normed = grad_sum_two + jnp.concatenate(grad_parts, axis=-1)
    grad_sum_one, scaling_grad, offsets_grad = norm_backward(
        grad_normed, unit_one, scale_one, scaling_full
    )
    grad_attended = behind(grad_sum_one.astype(low))
    output_grad = weight_term(joined, grad_attended)
    grad_joined = project_back(grad_attended, output_full)
    grad_context = grad_joined[..., :ATT].astype(low)
    grad_span_values, grad_mixconv, grad_conv_tokens, taps_grad, point_grad, depth_grad = (
        conv_back_call(
            lengths, tokens, grad_joined[..., ATT:], tap_weights, span_values, mixture, query,
            key_conv, depthwise, point_full, taps_full, depth_full,
        )
    )
    grad_mixconv = behind(grad_mixconv)
    taps_grad = taps_grad[:, : KERNEL * SLOTS].reshape(ATT, KERNEL, SLOTS)[..., :HEADS]
    taps_grad = taps_grad.swapaxes(1, 2)
    depth_grad = depth_grad[:KERNEL]
    small_terms = jnp.concatenate(
        [
            depth_grad.T,
            scaling_grad[:, None],
            offsets_grad[:, None],
            stretch_grad[:, None],
            displace_grad[:, None],
            taps_grad.reshape(D, -1),
        ],
        axis=1,
    )
    small_terms = jnp.pad(small_terms, ((0, 0), (0, 128 - used)))
    grad_query, grad_keys, grad_values = attend_back_call(
        lengths, query, keys, values, logsum, grad_context, grad_mixconv
    )
    grad_query = behind(grad_query)
    qk_grad = weight_term(masked, jnp.concatenate([grad_query, grad_keys], axis=-1))
    qk_grad = behind(qk_grad)
    vs_grad = weight_term(masked, jnp.concatenate([grad_values, grad_span_values], axis=-1))
    summed = links.reduce_two([qk_grad, point_grad, small_terms], [vs_grad, output_grad])
    grad_masked = (
        grad_sum_one
        + project_back(grad_query, query_full)
        + project_back(grad_keys, key_full)
        + project_back(grad_values, value_full)
        + project_back(grad_span_values, span_full)
        + grad_conv_tokens
    )
    tokens_grad = grad_masked * valid_rows[..., None]
    while not ended:
        behind(summed)
    small_sum = summed[:, 3 * ATT : 3 * ATT + 128]
    second_sum = summed[:, 3 * ATT + 128 :]
    return (
        activations,
        tokens_grad,
        summed[:, :ATT],
        summed[:, ATT : 2 * ATT],
        second_sum[:, :ATT],
        small_sum[:, :KERNEL].T,
        summed[:, 2 * ATT : 3 * ATT],
        small_sum[:, KERNEL + 4 : used].reshape(-1),
        second_sum[:, ATT : 2 * ATT],
        second_sum[:, 2 * ATT :],
        small_sum[:, KERNEL],
        small_sum[:, KERNEL + 1],
        jnp.stack([grouped_sum[:, D + g * wide : D + (g + 1) * wide].T for g in range(GROUPS)]),
        jnp.stack([grouped_sum[:, g * wide : (g + 1) * wide] for g in range(GROUPS)]),
        small_sum[:, KERNEL + 2],
        small_sum[:, KERNEL + 3],
    )


def solution(mesh):
    both = ("dp", "fsdp")
    weights = (
        P(both, None),
        P(both, None),
        P(both, None),
        P(None, both),
        P(both, None),
        P(both),
        P(both, None),
        P(both, None),
        P(both),
        P(both),
        P(None, None, both),
        P(None, both, None),
        P(both),
        P(both),
    )
    row = P(both, None, None)
    links = Links(mesh.shape["dp"], mesh.shape["fsdp"])

    def body(*args):
        return on_device(links, *args)

    return jax.shard_map(
        body,
        mesh=mesh,
        in_specs=(row, P(both)) + weights + (row,),
        out_specs=(row, row) + weights,
        check_vma=False,
    )
```

```python
import jax
import jax.numpy as jnp
from jax import lax
from jax.experimental import pallas as pl
from jax.experimental.pallas import tpu as pltpu
from jax.sharding import PartitionSpec as P

D = 768
HEADS = 6
HEAD = 64
KERNEL = 9
GROUPS = 2
ATT = 384

epsilon = 1e-06
masked_score = -1000000000.0
root_half = 0.7071067811865476
slope_factor = 0.3989422804014327


def weight_term(left, grad_out):
    return jnp.einsum("bsk,bsn->kn", left, grad_out, preferred_element_type=jnp.float32)


CHUNK = 128
HALO = 8
SLOTS = 8
WIDE = D // GROUPS


def dot(a, b):
    return jnp.dot(a, b, preferred_element_type=jnp.float32)


def dot_nt(a, b):
    return lax.dot_general(a, b, (((1,), (1,)), ((), ())), preferred_element_type=jnp.float32)


def dot_tn(a, b):
    return lax.dot_general(a, b, (((0,), (0,)), ((), ())), preferred_element_type=jnp.float32)


def lane_of(shape):
    return lax.broadcasted_iota(jnp.int32, shape, len(shape) - 1)


def row_of(shape):
    return lax.broadcasted_iota(jnp.int32, shape, len(shape) - 2)


def shifted(value, offset, count):
    if offset % 8:
        value = pltpu.roll(value, value.shape[0] - offset, axis=0)
        offset = 0
    return value[offset : offset + count]


def high_low(value):
    high = value.astype(jnp.bfloat16)
    low = (value - high.astype(jnp.float32)).astype(jnp.bfloat16)
    return jnp.concatenate([high, low], axis=1)


def over_taps(value, combine):
    for step in (8, 16, 32, 64):
        value = combine(value, pltpu.roll(value, step, axis=1))
    return value


def fill_spread(spread_ref):
    shape = (256, ATT)
    for m in range(KERNEL):
        lanes = row_of(shape) % 128
        head = lane_of(shape) // HEAD
        spread_ref[m] = jnp.where(lanes == m * SLOTS + head, 1.0, 0.0).astype(jnp.bfloat16)


def pad_rows(ref, length):
    zeros = jnp.zeros((HALO, ref.shape[1]), ref.dtype)
    ref[0:HALO, :] = zeros
    ref[HALO + length : 2 * HALO + length, :] = zeros


def small_turns():
    low = jnp.bfloat16
    rows = [
        jnp.where(lane_of((ATT, D)) == 2 * row_of((ATT, D)) + b, 1.0, 0.0).astype(low)
        for b in range(2)
    ]
    near, far = row_of((128, 128)), lane_of((128, 128))
    tap, head = far // SLOTS, far % SLOTS
    lanes = []
    for b in range(2):
        hit = (near == KERNEL + 4 + (head - 3 * b) * KERNEL + tap) & (tap < KERNEL)
        hit = hit & (head >= 3 * b) & (head < 3 * b + 3)
        lanes.append(jnp.where(hit, 1.0, 0.0).astype(low))
    return rows, lanes


def project_kernel(
    lengths_ref, tokens_ref, first_ref, second_ref,
    query_ref, keys_ref, values_ref, conv_ref, depthwise_ref, mixture_ref, tapw_ref, span_ref,
    vectors_ref, taps_ref, padded_ref,
):
    length = tokens_ref.shape[1]
    count = lengths_ref[pl.program_id(0)]
    low = jnp.bfloat16

    @pl.when(pl.program_id(0) == 0)
    def _():
        small = first_ref[:, 3 * ATT : 3 * ATT + 128]
        vectors_ref[...] = small.astype(jnp.float32).T[:16]
        rows, lanes = small_turns()
        total = None
        for b in range(2):
            part = dot(rows[b], dot(small, lanes[b]).astype(low))
            total = part if total is None else total + part
        taps_ref[...] = total.astype(low)

    pad_rows(padded_ref, length)
    tokens = tokens_ref[0]
    masked = jnp.where(row_of(tokens.shape) < count, tokens.astype(jnp.float32), 0.0)
    padded_ref[HALO : HALO + length, :] = masked
    masked = masked.astype(low)
    query_ref[0] = dot(masked, first_ref[:, :ATT]).astype(low)
    keys_ref[0] = dot(masked, first_ref[:, ATT : 2 * ATT]).astype(low)
    values_ref[0] = dot(masked, second_ref[:, :ATT]).astype(low)
    span_ref[0] = dot(masked, second_ref[:, ATT : 2 * ATT])

    def depth_chunk(i, carry):
        start = pl.multiple_of(i * CHUNK, CHUNK)
        block = padded_ref[pl.ds(start, CHUNK + 2 * HALO), :]
        total = None
        for m in range(KERNEL):
            term = shifted(block, HALO - KERNEL // 2 + m, CHUNK) * vectors_ref[m : m + 1, :]
            total = term if total is None else total + term
        depthwise_ref[0, pl.ds(start, CHUNK), :] = total.astype(low)
        return carry

    lax.fori_loop(0, length // CHUNK, depth_chunk, 0)
    conv = dot(depthwise_ref[0], first_ref[:, 2 * ATT : 3 * ATT])
    conv_ref[0] = conv
    mixture_ref[0] = (conv * query_ref[0].astype(jnp.float32)).astype(low)
    logits = dot(mixture_ref[0], taps_ref[...])
    logits = jnp.where(lane_of(logits.shape) < KERNEL * SLOTS, logits, -1e30)
    exponent = jnp.exp(logits - over_taps(logits, jnp.maximum))
    tapw_ref[0] = exponent / over_taps(exponent, jnp.add)


def span_kernel(tapw_ref, span_ref, out_ref, span_padded_ref, spread_ref):
    length = span_ref.shape[1]

    @pl.when(pl.program_id(0) == 0)
    def _():
        fill_spread(spread_ref)

    pad_rows(span_padded_ref, length)
    span_padded_ref[HALO : HALO + length, :] = span_ref[0]

    def span_chunk(i, carry):
        start = pl.multiple_of(i * CHUNK, CHUNK)
        block = span_padded_ref[pl.ds(start, CHUNK + 2 * HALO), :]
        both = high_low(tapw_ref[0, pl.ds(start, CHUNK), :])
        total = None
        for m in range(KERNEL):
            term = shifted(block, HALO - KERNEL // 2 + m, CHUNK) * dot(both, spread_ref[m])
            total = term if total is None else total + term
        out_ref[0, pl.ds(start, CHUNK), :] = total.astype(jnp.bfloat16)
        return carry

    lax.fori_loop(0, length // CHUNK, span_chunk, 0)


def attend_kernel(lengths_ref, query_ref, keys_ref, values_ref, context_ref, logsum_ref):
    length = query_ref.shape[1]
    count = lengths_ref[pl.program_id(0)]
    low = jnp.bfloat16
    rows = 256

    def attend_pair(index, carry):
        pair, half = index // (length // rows), index % (length // rows)
        lanes = pl.ds(pl.multiple_of(pair * 128, 128), 128)
        place = pl.ds(pl.multiple_of(half * rows, rows), rows)
        query = query_ref[0, place, lanes]
        keys = keys_ref[0, :, lanes]
        values = values_ref[0, :, lanes]
        left = lane_of((rows, 128)) < HEAD
        sums = logsum_ref[0, place, :]
        contexts = []
        for j in range(2):
            mine = left if j == 0 else jnp.logical_not(left)
            own = jnp.where(mine, query.astype(jnp.float32), 0.0).astype(low)
            scores = dot_nt(own, keys) * HEAD ** (-0.5)
            scores = jnp.where(lane_of(scores.shape) < count, scores, masked_score)
            highest = jnp.max(scores, axis=-1, keepdims=True)
            exponent = jnp.exp(scores - highest)
            totals = jnp.sum(exponent, axis=-1, keepdims=True)
            contexts.append(dot((exponent * (1.0 / totals)).astype(low), values))
            sums = jnp.where(lane_of(sums.shape) == pair * 2 + j, highest + jnp.log(totals), sums)
        logsum_ref[0, place, :] = sums
        context_ref[0, place, lanes] = jnp.where(left, contexts[0], contexts[1]).astype(low)
        return carry

    logsum_ref[0] = jnp.zeros(logsum_ref.shape[1:], jnp.float32)
    lax.fori_loop(0, (HEADS // 2) * (length // rows), attend_pair, 0)


def whole_spec(shape, single=False):
    mode = {"pipeline_mode": pl.Buffered(1)} if single else {}
    return pl.BlockSpec(shape, lambda i, *_: (0,) * len(shape), **mode)


def seq_spec(length, width):
    return pl.BlockSpec((1, length, width), lambda i, *_: (i, 0, 0))


LIMIT = pltpu.CompilerParams(vmem_limit_bytes=60 * 1024 * 1024, dimension_semantics=("arbitrary",))


def per_sequence(kernel, name, scalars, arrays, weights, outs, wholes, scratch, single=False):
    seqs, length = arrays[0].shape[:2]
    return pl.pallas_call(
        kernel,
        grid_spec=pltpu.PrefetchScalarGridSpec(
            num_scalar_prefetch=len(scalars),
            grid=(seqs,),
            in_specs=[seq_spec(length, a.shape[2]) for a in arrays]
            + [whole_spec(a.shape, single) for a in weights],
            out_specs=[seq_spec(length, w) for w, _ in outs] + [whole_spec(s) for s, _ in wholes],
            scratch_shapes=[pltpu.VMEM(s, t) for s, t in scratch],
        ),
        out_shape=[jax.ShapeDtypeStruct((seqs, length, w), t) for w, t in outs]
        + [jax.ShapeDtypeStruct(s, t) for s, t in wholes],
        compiler_params=LIMIT,
        name=name,
    )(*scalars, *arrays, *weights)


LOW, FULL = jnp.bfloat16, jnp.float32


def project_call(lengths, tokens, first, second):
    outs = [
        (ATT, LOW), (ATT, LOW), (ATT, LOW), (ATT, FULL), (D, LOW), (ATT, LOW), (128, FULL),
        (ATT, FULL),
    ]
    return per_sequence(
        project_kernel, "project", [lengths], [tokens], [first, second], outs,
        [((16, D), FULL), ((ATT, 128), LOW)], [((tokens.shape[1] + 2 * HALO, D), FULL)],
    )


def span_call(tapw, span):
    scratch = [((span.shape[1] + 2 * HALO, ATT), FULL), ((KERNEL, 256, ATT), LOW)]
    return per_sequence(span_kernel, "span", [], [tapw, span], [], [(ATT, LOW)], [], scratch)[0]


def attend_call(lengths, query, keys, values):
    outs = [(ATT, LOW), (128, FULL)]
    return per_sequence(
        attend_kernel, "attend", [lengths], [query, keys, values], [], outs, [], []
    )


def unit_of(value):
    mean = jnp.mean(value, axis=-1, keepdims=True)
    centered = value - mean
    scale = lax.rsqrt(jnp.mean(centered * centered, axis=-1, keepdims=True) + epsilon)
    return centered * scale, scale


def norm_back(grad_out, unit, scale, gain):
    scaled = grad_out * gain
    return scale * (
        scaled
        - jnp.mean(scaled, axis=-1, keepdims=True)
        - unit * jnp.mean(scaled * unit, axis=-1, keepdims=True)
    )


def feed_kernel(
    lengths_ref, tokens_ref, context_ref, span_ref, cotangent_ref, second_ref, part0_ref,
    part1_ref, part2_ref, part3_ref, vectors_ref,
    activations_ref, grad_one_ref, grad_context_ref, grad_span_ref, send_ref, keep_ref,
    output_grad_ref, vector_grad_ref,
    total_ref, active_ref, slope_ref, normed_ref, grad_ref,
):
    count = lengths_ref[pl.program_id(0)]
    low = jnp.bfloat16

    @pl.when(pl.program_id(0) == 0)
    def _():
        for ref in (total_ref, output_grad_ref, vector_grad_ref):
            ref[...] = jnp.zeros(ref.shape, jnp.float32)

    scaling, offsets, stretch, displace = (
        vectors_ref[KERNEL + i : KERNEL + i + 1, :] for i in range(4)
    )
    quarters = (part0_ref, part1_ref, part2_ref, part3_ref)
    tokens = tokens_ref[0]
    valid = row_of(tokens.shape) < count
    value = dot(context_ref[0], second_ref[:ATT, 2 * ATT :])
    value = value + dot(span_ref[0], second_ref[ATT:, 2 * ATT :])
    value = value + jnp.where(valid, tokens.astype(jnp.float32), 0.0)
    unit_one, scale_one = unit_of(value)
    normed_one = unit_one * scaling + offsets
    normed_ref[...] = normed_one.astype(low)
    parts = []
    for g in range(GROUPS):
        lanes = slice(g * WIDE, (g + 1) * WIDE)
        inner = slice(D + g * WIDE, D + (g + 1) * WIDE)
        total = None
        for h in range(4):
            units = slice(h * D // 2, (h + 1) * D // 2)
            hidden = dot_nt(normed_ref[:, lanes], quarters[h][:, inner])
            even = 0.5 * (1.0 + lax.erf(hidden * root_half))
            active_ref[g, :, units] = (hidden * even).astype(low)
            slope_ref[g, :, units] = even + hidden * jnp.exp(-0.5 * hidden * hidden) * slope_factor
            part = dot(active_ref[g, :, units], quarters[h][:, lanes])
            total = part if total is None else total + part
        parts.append(total)
    unit_two, scale_two = unit_of(jnp.concatenate(parts, axis=1) + normed_one)
    result = unit_two * stretch + displace
    activations_ref[0] = jnp.where(valid, result, 0.0).astype(low)
    grad = jnp.where(valid, cotangent_ref[0].astype(jnp.float32), 0.0)
    vector_grad_ref[2:3, :] += jnp.sum(grad * unit_two, axis=0, keepdims=True)
    vector_grad_ref[3:4, :] += jnp.sum(grad, axis=0, keepdims=True)
    grad_two = norm_back(grad, unit_two, scale_two, stretch)
    grad_ref[...] = grad_two.astype(low)
    parts = []
    for g in range(GROUPS):
        lanes = slice(g * WIDE, (g + 1) * WIDE)
        inner = slice(D + g * WIDE, D + (g + 1) * WIDE)
        total = None
        for h in range(4):
            units = slice(h * D // 2, (h + 1) * D // 2)
            total_ref[units, lanes] += dot_tn(active_ref[g, :, units], grad_ref[:, lanes])
            hidden = dot_nt(grad_ref[:, lanes], quarters[h][:, lanes]) * slope_ref[g, :, units]
            hidden = hidden.astype(low)
            total_ref[units, inner] += dot_tn(hidden, normed_ref[:, lanes])
            part = dot(hidden, quarters[h][:, inner])
            total = part if total is None else total + part
        parts.append(total)
    grad = grad_two + jnp.concatenate(parts, axis=1)
    vector_grad_ref[0:1, :] += jnp.sum(grad * unit_one, axis=0, keepdims=True)
    vector_grad_ref[1:2, :] += jnp.sum(grad, axis=0, keepdims=True)
    grad = norm_back(grad, unit_one, scale_one, scaling)
    grad_one_ref[0] = grad
    grad_ref[...] = grad.astype(low)
    output_grad_ref[:ATT, :] += dot_tn(context_ref[0], grad_ref[...])
    output_grad_ref[ATT:, :] += dot_tn(span_ref[0], grad_ref[...])
    grad_context_ref[0] = dot_nt(grad_ref[...], second_ref[:ATT, 2 * ATT :]).astype(low)
    grad_span_ref[0] = dot_nt(grad_ref[...], second_ref[ATT:, 2 * ATT :])

    @pl.when(pl.program_id(0) == pl.num_programs(0) - 1)
    def _():
        for h in range(2):
            keep_ref[h] = total_ref[h * D : h * D + D // 2, :]
            send_ref[h] = total_ref[h * D + D // 2 : (h + 1) * D, :].astype(low)


def feed_call(lengths, tokens, context, span, cotangent, second, quarters, vectors):
    length = tokens.shape[1]
    outs = [(D, LOW), (D, FULL), (ATT, LOW), (ATT, FULL)]
    wholes = [
        ((2, D // 2, 2 * D), LOW), ((2, D // 2, 2 * D), FULL), ((D, D), FULL), ((8, D), FULL),
    ]
    scratch = [
        ((2 * D, 2 * D), FULL), ((2, length, 2 * D), LOW), ((2, length, 2 * D), FULL), ((length, D), LOW),
        ((length, D), LOW),
    ]
    return per_sequence(
        feed_kernel, "feed", [lengths], [tokens, context, span, cotangent],
        [second, *quarters, vectors], outs, wholes, scratch, single=True,
    )


def tokens_kernel(
    lengths_ref, query_ref, keys_ref, values_ref, span_ref, one_ref, conv_ref, first_ref,
    second_ref, out_ref,
):
    count = lengths_ref[pl.program_id(0)]
    total = one_ref[0] + conv_ref[0]
    total = total + dot_nt(query_ref[0], first_ref[:, :ATT])
    total = total + dot_nt(keys_ref[0], first_ref[:, ATT : 2 * ATT])
    total = total + dot_nt(values_ref[0], second_ref[:, :ATT])
    total = total + dot_nt(span_ref[0], second_ref[:, ATT : 2 * ATT])
    out_ref[0] = jnp.where(row_of(total.shape) < count, total, 0.0)


def tokens_call(lengths, grads, first, second):
    return per_sequence(
        tokens_kernel, "tokens_grad", [lengths], grads, [first, second], [(D, FULL)], [], []
    )[0]


def span_back_kernel(
    grad_span_ref, tapw_ref, span_ref, mixture_ref, query_ref, conv_ref, taps_ref,
    grad_spanv_ref, grad_mixconv_ref, grad_conv_ref, taps_grad_ref,
    span_padded_ref, grad_padded_ref, tapw_padded_ref, logit_ref, spread_ref, gather_ref,
):
    length = span_ref.shape[1]
    low = jnp.bfloat16

    @pl.when(pl.program_id(0) == 0)
    def _():
        fill_spread(spread_ref)
        shape = (ATT, 128)
        for m in range(KERNEL):
            hit = lane_of(shape) == m * SLOTS + row_of(shape) // HEAD
            gather_ref[m] = jnp.where(hit, 1.0, 0.0).astype(low)
        taps_grad_ref[...] = jnp.zeros(taps_grad_ref.shape, jnp.float32)

    inside = slice(HALO, HALO + length)
    for ref in (span_padded_ref, grad_padded_ref, tapw_padded_ref):
        pad_rows(ref, length)
    span_padded_ref[inside, :] = span_ref[0]
    grad_padded_ref[inside, :] = grad_span_ref[0]
    tapw_padded_ref[inside, :] = tapw_ref[0]

    def span_chunk(i, carry):
        start = pl.multiple_of(i * CHUNK, CHUNK)
        place = pl.ds(start, CHUNK)
        around = pl.ds(start, CHUNK + 2 * HALO)
        spans = span_padded_ref[around, :]
        grads = grad_padded_ref[around, :]
        both = high_low(tapw_padded_ref[around, :])
        own = grads[HALO : HALO + CHUNK]
        grad_taps = None
        total = None
        for m in range(KERNEL):
            product = shifted(spans, HALO - KERNEL // 2 + m, CHUNK) * own
            part = dot(product.astype(low), gather_ref[m])
            grad_taps = part if grad_taps is None else grad_taps + part
            spread = dot(both, spread_ref[m]) * grads
            term = shifted(spread, HALO + KERNEL // 2 - m, CHUNK)
            total = term if total is None else total + term
        grad_spanv_ref[0, place, :] = total.astype(low)
        weights = tapw_ref[0, place, :]
        centre = over_taps(weights * grad_taps, jnp.add)
        logit_ref[place, :] = (weights * (grad_taps - centre)).astype(low)
        return carry

    lax.fori_loop(0, length // CHUNK, span_chunk, 0)
    grad_logits = logit_ref[...]
    taps_grad_ref[...] += dot_tn(mixture_ref[0], grad_logits)
    grad_mixture = dot_nt(grad_logits, taps_ref[...])
    grad_conv_ref[0] = (grad_mixture * query_ref[0].astype(jnp.float32)).astype(low)
    grad_mixconv_ref[0] = grad_mixture * conv_ref[0]


def span_back_call(grad_span, tapw, span, mixture, query, conv, taps):
    length = span.shape[1]
    rows = length + 2 * HALO
    return per_sequence(
        span_back_kernel, "span_back", [],
        [grad_span, tapw, span, mixture, query, conv], [taps],
        [(ATT, LOW), (ATT, FULL), (ATT, LOW)], [((ATT, 128), FULL)],
        [
            ((rows, ATT), FULL), ((rows, ATT), FULL), ((rows, 128), FULL), ((length, 128), LOW),
            ((KERNEL, 256, ATT), LOW), ((KERNEL, ATT, 128), LOW),
        ],
    )


def depth_back_kernel(
    lengths_ref, tokens_ref, grad_conv_ref, depthwise_ref, first_ref, vectors_ref, taps_grad_ref,
    vector_grad_ref,
    grad_tokens_ref, point_grad_ref, small_ref, padded_ref, back_padded_ref, sums_ref,
):
    length = tokens_ref.shape[1]
    count = lengths_ref[pl.program_id(0)]
    low = jnp.bfloat16

    @pl.when(pl.program_id(0) == 0)
    def _():
        point_grad_ref[...] = jnp.zeros(point_grad_ref.shape, jnp.float32)
        sums_ref[...] = jnp.zeros(sums_ref.shape, jnp.float32)

    inside = slice(HALO, HALO + length)
    for ref in (padded_ref, back_padded_ref):
        pad_rows(ref, length)
    tokens = tokens_ref[0]
    padded_ref[inside, :] = jnp.where(row_of(tokens.shape) < count, tokens.astype(jnp.float32), 0.0)
    point_grad_ref[...] += dot_tn(depthwise_ref[0], grad_conv_ref[0])
    back_padded_ref[inside, :] = dot_nt(grad_conv_ref[0], first_ref[:, 2 * ATT : 3 * ATT])

    def depth_chunk(i, carry):
        start = pl.multiple_of(i * CHUNK, CHUNK)
        around = pl.ds(start, CHUNK + 2 * HALO)
        tokens = padded_ref[around, :]
        grads = back_padded_ref[around, :]
        own = grads[HALO : HALO + CHUNK]
        total = None
        for m in range(KERNEL):
            product = shifted(tokens, HALO - KERNEL // 2 + m, CHUNK) * own
            part = product[0:8]
            for r in range(8, CHUNK, 8):
                part = part + product[r : r + 8]
            sums_ref[m * 8 : m * 8 + 8, :] += part
            term = shifted(grads, HALO + KERNEL // 2 - m, CHUNK) * vectors_ref[m : m + 1, :]
            total = term if total is None else total + term
        grad_tokens_ref[0, pl.ds(start, CHUNK), :] = total
        return carry

    lax.fori_loop(0, length // CHUNK, depth_chunk, 0)

    @pl.when(pl.program_id(0) == pl.num_programs(0) - 1)
    def _():
        depth_grad = [
            jnp.sum(sums_ref[m * 8 : m * 8 + 8, :], axis=0, keepdims=True) for m in range(KERNEL)
        ]
        vector_grad = [vector_grad_ref[i : i + 1, :] for i in range(4)]
        filler = [jnp.zeros((128 - KERNEL - 4, D), jnp.float32)]
        total = jnp.concatenate(depth_grad + vector_grad + filler, axis=0).T
        rows, lanes = small_turns()
        grad = taps_grad_ref[...]
        high = grad.astype(low)
        rest = (grad - high.astype(jnp.float32)).astype(low)
        for b in range(2):
            for part in (high, rest):
                moved = dot_nt(part, lanes[b]).astype(low)
                total = total + dot_tn(rows[b], moved)
        small_ref[...] = total


def depth_back_call(lengths, tokens, grad_conv, depthwise, first, vectors, taps_grad, vector_grad):
    rows = tokens.shape[1] + 2 * HALO
    return per_sequence(
        depth_back_kernel, "depth_back", [lengths], [tokens, grad_conv, depthwise],
        [first, vectors, taps_grad, vector_grad], [(D, FULL)],
        [((D, ATT), FULL), ((D, 128), FULL)],
        [((rows, D), FULL), ((rows, D), FULL), ((KERNEL * 8, D), FULL)],
    )


def attend_back_kernel(
    lengths_ref, query_ref, keys_ref, values_ref, logsum_ref, grad_context_ref, mixconv_ref,
    grad_query_ref, grad_keys_ref, grad_values_ref,
    turned_ref, keys_sum_ref, values_sum_ref,
):
    length = query_ref.shape[1]
    count = lengths_ref[pl.program_id(0)]
    low = jnp.bfloat16
    factor = HEAD ** (-0.5)
    turned_ref[...] = logsum_ref[0].T
    keys_sum_ref[...] = jnp.zeros(keys_sum_ref.shape, jnp.float32)
    values_sum_ref[...] = jnp.zeros(values_sum_ref.shape, jnp.float32)
    part = 256

    for pair in range(HEADS // 2):
        lanes = slice(pair * 128, pair * 128 + 128)

        def chunk(i, carry, pair=pair, lanes=lanes):
            place = pl.ds(pl.multiple_of(i * part, part), part)
            keys = keys_ref[0, :, lanes]
            values = values_ref[0, :, lanes]
            query = query_ref[0, place, lanes].astype(jnp.float32)
            grads = grad_context_ref[0, place, lanes].astype(jnp.float32)
            total = mixconv_ref[0, place, lanes]
            for j in range(2):
                own = lane_of((part, 128)) // HEAD == j
                query_j = jnp.where(own, query, 0.0).astype(low)
                grads_j = jnp.where(own, grads, 0.0).astype(low)
                scores = dot_nt(keys, query_j) * factor
                attention = jnp.exp(scores - turned_ref[pair * 2 + j : pair * 2 + j + 1, place])
                attention = jnp.where(row_of(scores.shape) < count, attention, 0.0)
                grad_attention = dot_nt(values, grads_j)
                values_sum_ref[:, lanes] += dot(attention.astype(low), grads_j)
                centre = jnp.sum(attention * grad_attention, axis=0, keepdims=True)
                grad_scores = (attention * (grad_attention - centre)).astype(low)
                keys_sum_ref[:, lanes] += dot(grad_scores, query_j)
                both = dot_tn(grad_scores, keys)
                total = total + jnp.where(own, both, 0.0) * factor
            grad_query_ref[0, place, lanes] = total.astype(low)
            return carry

        lax.fori_loop(0, length // part, chunk, 0)
    grad_keys_ref[0] = (keys_sum_ref[...] * factor).astype(low)
    grad_values_ref[0] = values_sum_ref[...].astype(low)


def attend_back_call(lengths, query, keys, values, logsum, grad_context, mixconv):
    length = query.shape[1]
    return per_sequence(
        attend_back_kernel, "attend_back", [lengths],
        [query, keys, values, logsum, grad_context, mixconv], [], [(ATT, LOW)] * 3, [],
        [((128, length), FULL), ((length, ATT), FULL), ((length, ATT), FULL)],
    )


class Links:
    def __init__(self, dp, fsdp):
        self.sizes = {"dp": dp, "fsdp": fsdp}
        self.outer = [("dp", 1 << i) for i in range(32) if (1 << i) < dp][::-1]
        inner = [("fsdp", 1 << i) for i in range(1, 32) if (1 << i) < fsdp]
        core = [("fsdp", 1)] if fsdp > 1 else []
        self.tails = (inner + core, inner[::-1] + core)
        self.count = dp * fsdp
        self.named = self.outer + [("fsdp", 1 << i) for i in range(32) if (1 << i) < fsdp][::-1]

    def weight(self, stage):
        axis, bit = stage
        return bit * self.sizes["fsdp"] if axis == "dp" else bit

    def swap(self, value, stage):
        axis, bit = stage
        return lax.ppermute(value, axis, [(i, i ^ bit) for i in range(self.sizes[axis])])

    def slots_of_owners(self, order):
        me = lax.axis_index("dp") * self.sizes["fsdp"] + lax.axis_index("fsdp")
        rel = jnp.arange(self.count, dtype=jnp.int32) ^ me
        slot = jnp.zeros_like(rel)
        for k, stage in enumerate(self.outer + self.tails[order]):
            slot = slot + jnp.where((rel & self.weight(stage)) != 0, 1 << k, 0)
        return slot

    def owners(self, slots, order):
        taken = jnp.take(slots, self.slots_of_owners(order), axis=0, mode="clip")
        return taken.reshape(-1, slots.shape[-1])

    def gather_outer(self, shards):
        blocks = jnp.concatenate(shards, axis=1)[None]
        for stage in self.outer:
            blocks = jnp.concatenate([blocks, self.swap(blocks, stage)], axis=0)
        parts, start = [], 0
        for shard in shards:
            parts.append(blocks[..., start : start + shard.shape[1]])
            start += shard.shape[1]
        return parts

    def gather_tails(self, parts):
        for stages in zip(*self.tails):
            parts = [jnp.concatenate(part, axis=0) for part in parts]
            parts = [[part, self.swap(part, stage)] for part, stage in zip(parts, stages)]
            parts = yield parts

    def reduce_slots(self, send, keep):
        stages = [list(pair) for pair in zip(*self.tails)][::-1] + [[s, s] for s in self.outer[::-1]]
        for k, pair in enumerate(stages):
            if k > 0:
                half = keep.shape[1] // 2
                send, keep = keep[:, half:].astype(jnp.bfloat16), keep[:, :half]
            if pair[0] == pair[1]:
                got = self.swap(send, pair[0])
            else:
                got = jnp.stack([self.swap(send[i], pair[i]) for i in range(2)])
            keep = yield keep + got.astype(jnp.float32)

    def split(self, terms, left, stage):
        axis, bit = stage
        dim = left.index(stage)
        mine = (lax.axis_index(axis) // bit) & 1
        send = [
            lax.dynamic_index_in_dim(t, 1 - mine, dim, keepdims=False).astype(jnp.bfloat16)
            for t in terms
        ]
        keep = [lax.dynamic_index_in_dim(t, mine, dim, keepdims=False) for t in terms]
        return jnp.concatenate(send, axis=-1), jnp.concatenate(keep, axis=-1)

    def reduce_owners(self, first, second):
        lists = [
            [t.reshape((2,) * len(self.named) + (-1, t.shape[-1])) for t in terms]
            for terms in (first, second)
        ]
        lefts = [list(self.named), list(self.named)]
        for pair in [list(pair) for pair in zip(*self.tails)][::-1]:
            halves = [self.split(lists[i], lefts[i], pair[i]) for i in range(2)]
            if pair[0] == pair[1]:
                cut = halves[0][0].shape[-1]
                got = self.swap(jnp.concatenate([halves[0][0], halves[1][0]], axis=-1), pair[0])
                got = [got[..., :cut], got[..., cut:]]
            else:
                got = [self.swap(halves[i][0], pair[i]) for i in range(2)]
            for i in range(2):
                lists[i] = [halves[i][1] + got[i].astype(jnp.float32)]
                lefts[i].remove(pair[i])
            lists = yield lists
        total, left = [lists[0][0], lists[1][0]], lefts[0]
        for stage in self.outer[::-1]:
            send, keep = self.split(total, left, stage)
            total = [keep + self.swap(send, stage).astype(jnp.float32)]
            left.remove(stage)
            total = yield total


class Staged:
    def __init__(self, stages):
        self.stages = stages
        self.value = next(stages)
        self.ended = False

    def behind(self, value):
        value = self.meet(value)
        self.step()
        return value

    def meet(self, value):
        if not self.ended:
            value, self.value = lax.optimization_barrier((value, self.value))
        return value

    def step(self):
        if not self.ended:
            try:
                self.value = self.stages.send(self.value)
            except StopIteration:
                self.ended = True

    def finish(self):
        while not self.ended:
            self.step()
        return self.value


def on_device(
    links,
    tokens,
    lengths,
    query_weight,
    key_weight,
    value_weight,
    depth_weight,
    point_weight,
    taps_weight,
    span_weight,
    output_weight,
    scaling,
    offsets,
    inner_weight,
    outer_weight,
    stretch,
    displace,
    cotangent,
):
    rows = query_weight.shape[0]
    packed = jnp.concatenate(
        [
            depth_weight.T,
            scaling[:, None],
            offsets[:, None],
            stretch[:, None],
            displace[:, None],
            taps_weight.reshape(rows, -1),
        ],
        axis=1,
    )
    used = packed.shape[1]
    packed = jnp.pad(packed, ((0, 0), (0, 128 - used)))
    grouped = jnp.concatenate(
        [outer_weight[0], outer_weight[1], inner_weight[0].T, inner_weight[1].T], axis=1
    )
    parts = links.gather_outer(
        [
            jnp.concatenate([query_weight, key_weight, point_weight, packed], axis=1),
            jnp.concatenate([value_weight, span_weight, output_weight], axis=1),
            grouped[:rows],
            grouped[rows:],
        ]
    )
    slots = Staged(links.gather_tails([[part] for part in parts[:2]])).finish()
    first, second = (links.owners(jnp.concatenate(slots[i], axis=0), i) for i in range(2))
    first, second, parts = lax.optimization_barrier((first, second, parts[2:]))
    gathering = Staged(links.gather_tails([[part] for part in parts]))

    (
        query, keys, values, key_conv, depthwise, mixture, tap_weights, span_values, vectors, taps,
    ) = project_call(lengths, tokens, first, second)
    query = gathering.behind(query)
    context, logsum = attend_call(lengths, query, keys, values)
    tap_weights, context = gathering.behind((tap_weights, context))
    span_output = span_call(tap_weights, span_values)
    span_output = gathering.behind(span_output)
    quarters = [piece.reshape(D // 2, 2 * D) for half in gathering.finish() for piece in half]

    (
        activations, grad_one, grad_context, grad_span, send, keep, output_grad, vector_grad,
    ) = feed_call(lengths, tokens, context, span_output, cotangent, second, quarters, vectors)
    reducing = Staged(links.reduce_slots(send, keep))
    grad_span_values, grad_mixconv, grad_conv, taps_grad = span_back_call(
        grad_span, tap_weights, span_values, mixture, query, key_conv, taps
    )
    grad_conv = reducing.behind(grad_conv)
    grad_shifted, point_grad, small_grad = depth_back_call(
        lengths, tokens, grad_conv, depthwise, first, vectors, taps_grad, vector_grad
    )
    grad_mixconv, grad_shifted = reducing.behind((grad_mixconv, grad_shifted))
    grad_query, grad_keys, grad_values = attend_back_call(
        lengths, query, keys, values, logsum, grad_context, grad_mixconv
    )
    grad_query = reducing.behind(grad_query)
    positions = lax.broadcasted_iota(jnp.int32, tokens.shape[:2], 1)
    masked = tokens * (positions < lengths[:, None]).astype(tokens.dtype)[..., None]
    qk_grad = weight_term(masked, jnp.concatenate([grad_query, grad_keys], axis=-1))
    vs_grad = weight_term(masked, jnp.concatenate([grad_values, grad_span_values], axis=-1))
    qk_grad, vs_grad = reducing.behind((qk_grad, vs_grad))
    summing = Staged(links.reduce_owners([qk_grad, point_grad, small_grad], [vs_grad, output_grad]))
    summing.value = reducing.behind(summing.value)
    grouped_sum = reducing.finish().reshape(-1, 2 * D)
    grad_one = summing.behind(grad_one)
    tokens_grad = tokens_call(
        lengths,
        [grad_query, grad_keys, grad_values, grad_span_values, grad_one, grad_shifted],
        first,
        second,
    )
    tokens_grad = summing.meet(tokens_grad)
    summed = summing.finish()[0]
    wide = WIDE
    small_sum = summed[:, 3 * ATT : 3 * ATT + 128]
    second_sum = summed[:, 3 * ATT + 128 :]
    return (
        activations,
        tokens_grad,
        summed[:, :ATT],
        summed[:, ATT : 2 * ATT],
        second_sum[:, :ATT],
        small_sum[:, :KERNEL].T,
        summed[:, 2 * ATT : 3 * ATT],
        small_sum[:, KERNEL + 4 : used].reshape(-1),
        second_sum[:, ATT : 2 * ATT],
        second_sum[:, 2 * ATT :],
        small_sum[:, KERNEL],
        small_sum[:, KERNEL + 1],
        jnp.stack([grouped_sum[:, D + g * wide : D + (g + 1) * wide].T for g in range(GROUPS)]),
        jnp.stack([grouped_sum[:, g * wide : (g + 1) * wide] for g in range(GROUPS)]),
        small_sum[:, KERNEL + 2],
        small_sum[:, KERNEL + 3],
    )


def solution(mesh):
    both = ("dp", "fsdp")
    weights = (
        P(both, None),
        P(both, None),
        P(both, None),
        P(None, both),
        P(both, None),
        P(both),
        P(both, None),
        P(both, None),
        P(both),
        P(both),
        P(None, None, both),
        P(None, both, None),
        P(both),
        P(both),
    )
    row = P(both, None, None)
    links = Links(mesh.shape["dp"], mesh.shape["fsdp"])

    def body(*args):
        return on_device(links, *args)

    return jax.shard_map(
        body,
        mesh=mesh,
        in_specs=(row, P(both)) + weights + (row,),
        out_specs=(row, row) + weights,
        check_vma=False,
    )
```

```python
import functools

import jax
import jax.numpy as jnp
from jax import lax
from jax.experimental import pallas as pl
from jax.experimental.pallas import tpu as pltpu
from jax.sharding import PartitionSpec as P

D = 768
HEADS = 6
HEAD = 64
KERNEL = 9
GROUPS = 2
ATT = 384

epsilon = 1e-06
masked_score = -1000000000.0
root_half = 0.7071067811865476
slope_factor = 0.3989422804014327


def weight_term(left, grad_out):
    return jnp.einsum("bsk,bsn->kn", left, grad_out, preferred_element_type=jnp.float32)


CHUNK = 128
CUTS = 2
HALO = 8
SLOTS = 8
WIDE = D // GROUPS


def dot(a, b):
    return jnp.dot(a, b, preferred_element_type=jnp.float32)


def dot_nt(a, b):
    return lax.dot_general(a, b, (((1,), (1,)), ((), ())), preferred_element_type=jnp.float32)


def dot_tn(a, b):
    return lax.dot_general(a, b, (((0,), (0,)), ((), ())), preferred_element_type=jnp.float32)


def lane_of(shape):
    return lax.broadcasted_iota(jnp.int32, shape, len(shape) - 1)


def row_of(shape):
    return lax.broadcasted_iota(jnp.int32, shape, len(shape) - 2)


def shifted(value, offset, count):
    if offset % 8:
        value = pltpu.roll(value, value.shape[0] - offset, axis=0)
        offset = 0
    return value[offset : offset + count]


def high_low(value):
    high = value.astype(jnp.bfloat16)
    low = (value - high.astype(jnp.float32)).astype(jnp.bfloat16)
    return jnp.concatenate([high, low], axis=1)


def over_taps(value, combine):
    for step in (8, 16, 32, 64):
        value = combine(value, pltpu.roll(value, step, axis=1))
    return value


def fill_spread(spread_ref):
    shape = (256, ATT)
    for m in range(KERNEL):
        lanes = row_of(shape) % 128
        head = lane_of(shape) // HEAD
        spread_ref[m] = jnp.where(lanes == m * SLOTS + head, 1.0, 0.0).astype(jnp.bfloat16)


def pad_rows(ref, length):
    zeros = jnp.zeros((HALO, ref.shape[1]), ref.dtype)
    ref[0:HALO, :] = zeros
    ref[HALO + length : 2 * HALO + length, :] = zeros


def small_turns():
    low = jnp.bfloat16
    rows = [
        jnp.where(lane_of((ATT, D)) == 2 * row_of((ATT, D)) + b, 1.0, 0.0).astype(low)
        for b in range(2)
    ]
    near, far = row_of((128, 128)), lane_of((128, 128))
    tap, head = far // SLOTS, far % SLOTS
    lanes = []
    for b in range(2):
        hit = (near == KERNEL + 4 + (head - 3 * b) * KERNEL + tap) & (tap < KERNEL)
        hit = hit & (head >= 3 * b) & (head < 3 * b + 3)
        lanes.append(jnp.where(hit, 1.0, 0.0).astype(low))
    return rows, lanes


def project_kernel(
    lengths_ref, tokens_ref, first_ref, second_ref,
    query_ref, keys_ref, values_ref, conv_ref, depthwise_ref, mixture_ref, tapw_ref, span_ref,
    vectors_ref, taps_ref, padded_ref,
):
    length = tokens_ref.shape[1]
    count = lengths_ref[pl.program_id(0)]
    low = jnp.bfloat16

    @pl.when(pl.program_id(0) == 0)
    def _():
        small = first_ref[:, 3 * ATT : 3 * ATT + 128]
        vectors_ref[...] = small.astype(jnp.float32).T[:16]
        rows, lanes = small_turns()
        total = None
        for b in range(2):
            part = dot(rows[b], dot(small, lanes[b]).astype(low))
            total = part if total is None else total + part
        taps_ref[...] = total.astype(low)

    pad_rows(padded_ref, length)
    tokens = tokens_ref[0]
    masked = jnp.where(row_of(tokens.shape) < count, tokens.astype(jnp.float32), 0.0)
    padded_ref[HALO : HALO + length, :] = masked
    masked = masked.astype(low)
    query_ref[0] = dot(masked, first_ref[:, :ATT]).astype(low)
    keys_ref[0] = dot(masked, first_ref[:, ATT : 2 * ATT]).astype(low)
    values_ref[0] = dot(masked, second_ref[:, :ATT]).astype(low)
    span_ref[0] = dot(masked, second_ref[:, ATT : 2 * ATT])

    def depth_chunk(i, carry):
        start = pl.multiple_of(i * CHUNK, CHUNK)
        block = padded_ref[pl.ds(start, CHUNK + 2 * HALO), :]
        total = None
        for m in range(KERNEL):
            term = shifted(block, HALO - KERNEL // 2 + m, CHUNK) * vectors_ref[m : m + 1, :]
            total = term if total is None else total + term
        depthwise_ref[0, pl.ds(start, CHUNK), :] = total.astype(low)
        return carry

    lax.fori_loop(0, length // CHUNK, depth_chunk, 0)
    conv = dot(depthwise_ref[0], first_ref[:, 2 * ATT : 3 * ATT])
    conv_ref[0] = conv
    mixture_ref[0] = (conv * query_ref[0].astype(jnp.float32)).astype(low)
    logits = dot(mixture_ref[0], taps_ref[...])
    logits = jnp.where(lane_of(logits.shape) < KERNEL * SLOTS, logits, -1e30)
    exponent = jnp.exp(logits - over_taps(logits, jnp.maximum))
    tapw_ref[0] = exponent / over_taps(exponent, jnp.add)


def span_kernel(tapw_ref, span_ref, out_ref, span_padded_ref, spread_ref):
    length = span_ref.shape[1]

    @pl.when(pl.program_id(0) == 0)
    def _():
        fill_spread(spread_ref)

    pad_rows(span_padded_ref, length)
    span_padded_ref[HALO : HALO + length, :] = span_ref[0]

    def span_chunk(i, carry):
        start = pl.multiple_of(i * CHUNK, CHUNK)
        block = span_padded_ref[pl.ds(start, CHUNK + 2 * HALO), :]
        both = high_low(tapw_ref[0, pl.ds(start, CHUNK), :])
        total = None
        for m in range(KERNEL):
            term = shifted(block, HALO - KERNEL // 2 + m, CHUNK) * dot(both, spread_ref[m])
            total = term if total is None else total + term
        out_ref[0, pl.ds(start, CHUNK), :] = total.astype(jnp.bfloat16)
        return carry

    lax.fori_loop(0, length // CHUNK, span_chunk, 0)


def attend_kernel(lengths_ref, query_ref, keys_ref, values_ref, context_ref, logsum_ref):
    length = query_ref.shape[1]
    count = lengths_ref[pl.program_id(0)]
    low = jnp.bfloat16
    rows = 256

    def attend_pair(index, carry):
        pair, half = index // (length // rows), index % (length // rows)
        lanes = pl.ds(pl.multiple_of(pair * 128, 128), 128)
        place = pl.ds(pl.multiple_of(half * rows, rows), rows)
        query = query_ref[0, place, lanes]
        keys = keys_ref[0, :, lanes]
        values = values_ref[0, :, lanes]
        left = lane_of((rows, 128)) < HEAD
        sums = logsum_ref[0, place, :]
        contexts = []
        for j in range(2):
            mine = left if j == 0 else jnp.logical_not(left)
            own = jnp.where(mine, query.astype(jnp.float32), 0.0).astype(low)
            scores = dot_nt(own, keys) * HEAD ** (-0.5)
            scores = jnp.where(lane_of(scores.shape) < count, scores, masked_score)
            highest = jnp.max(scores, axis=-1, keepdims=True)
            exponent = jnp.exp(scores - highest)
            totals = jnp.sum(exponent, axis=-1, keepdims=True)
            contexts.append(dot((exponent * (1.0 / totals)).astype(low), values))
            sums = jnp.where(lane_of(sums.shape) == pair * 2 + j, highest + jnp.log(totals), sums)
        logsum_ref[0, place, :] = sums
        context_ref[0, place, lanes] = jnp.where(left, contexts[0], contexts[1]).astype(low)
        return carry

    logsum_ref[0] = jnp.zeros(logsum_ref.shape[1:], jnp.float32)
    lax.fori_loop(0, (HEADS // 2) * (length // rows), attend_pair, 0)


def whole_spec(shape, single=False):
    mode = {"pipeline_mode": pl.Buffered(1)} if single else {}
    return pl.BlockSpec(shape, lambda i, *_: (0,) * len(shape), **mode)


def seq_spec(length, width, cuts=1):
    return pl.BlockSpec((1, length // cuts, width), lambda i, *_: (i // cuts, i % cuts, 0))


LIMIT = pltpu.CompilerParams(vmem_limit_bytes=60 * 1024 * 1024, dimension_semantics=("arbitrary",))


def one_sequence(kernel, name, index, scalars, arrays, outs, scratch, filled):
    seqs, length = arrays[0].shape[:2]

    def spec(width):
        return pl.BlockSpec((1, length, width), lambda i, *_: (index, 0, 0))

    inputs = len(scalars) + len(arrays)
    return pl.pallas_call(
        functools.partial(kernel, index),
        grid_spec=pltpu.PrefetchScalarGridSpec(
            num_scalar_prefetch=len(scalars),
            grid=(1,),
            in_specs=[spec(a.shape[2]) for a in arrays]
            + [pl.BlockSpec(memory_space=pl.ANY) for _ in filled],
            out_specs=[spec(w) for w, _ in outs],
            scratch_shapes=[pltpu.VMEM(s, t) for s, t in scratch],
        ),
        out_shape=[jax.ShapeDtypeStruct((seqs, length, w), t) for w, t in outs],
        input_output_aliases={inputs + i: i for i in range(len(filled))},
        compiler_params=LIMIT,
        name=name,
    )(*scalars, *arrays, *filled)


def per_sequence(
    kernel, name, scalars, arrays, weights, outs, wholes, scratch, single=False, cuts=1
):
    seqs, length = arrays[0].shape[:2]
    return pl.pallas_call(
        kernel,
        grid_spec=pltpu.PrefetchScalarGridSpec(
            num_scalar_prefetch=len(scalars),
            grid=(seqs * cuts,),
            in_specs=[seq_spec(length, a.shape[2], cuts) for a in arrays]
            + [whole_spec(a.shape, single) for a in weights],
            out_specs=[seq_spec(length, w, cuts) for w, _ in outs]
            + [whole_spec(s, single) for s, _ in wholes],
            scratch_shapes=[pltpu.VMEM(s, t) for s, t in scratch],
        ),
        out_shape=[jax.ShapeDtypeStruct((seqs, length, w), t) for w, t in outs]
        + [jax.ShapeDtypeStruct(s, t) for s, t in wholes],
        compiler_params=LIMIT,
        name=name,
    )(*scalars, *arrays, *weights)


LOW, FULL = jnp.bfloat16, jnp.float32


def project_call(lengths, tokens, first, second):
    outs = [
        (ATT, LOW), (ATT, LOW), (ATT, LOW), (ATT, FULL), (D, LOW), (ATT, LOW), (128, FULL),
        (ATT, FULL),
    ]
    return per_sequence(
        project_kernel, "project", [lengths], [tokens], [first, second], outs,
        [((16, D), FULL), ((ATT, 128), LOW)], [((tokens.shape[1] + 2 * HALO, D), FULL)],
    )


def span_call(tapw, span):
    scratch = [((span.shape[1] + 2 * HALO, ATT), FULL), ((KERNEL, 256, ATT), LOW)]
    return per_sequence(span_kernel, "span", [], [tapw, span], [], [(ATT, LOW)], [], scratch)[0]


def attend_call(lengths, query, keys, values):
    outs = [(ATT, LOW), (128, FULL)]
    return per_sequence(
        attend_kernel, "attend", [lengths], [query, keys, values], [], outs, [], []
    )


def unit_of(value):
    mean = jnp.mean(value, axis=-1, keepdims=True)
    centered = value - mean
    scale = lax.rsqrt(jnp.mean(centered * centered, axis=-1, keepdims=True) + epsilon)
    return centered * scale, scale


def norm_back(grad_out, unit, scale, gain):
    scaled = grad_out * gain
    return scale * (
        scaled
        - jnp.mean(scaled, axis=-1, keepdims=True)
        - unit * jnp.mean(scaled * unit, axis=-1, keepdims=True)
    )


def feed_kernel(
    lengths_ref, tokens_ref, context_ref, span_ref, cotangent_ref, second_ref, part0_ref,
    part1_ref, part2_ref, part3_ref, vectors_ref,
    activations_ref, grad_one_ref, grad_context_ref, grad_span_ref, send_ref, keep_ref,
    output_grad_ref, vector_grad_ref,
    slope_ref, active_ref, hidden_ref, normed_ref, grad_ref, attended_ref, joined_ref,
):
    length = tokens_ref.shape[1]
    count = lengths_ref[pl.program_id(0) // CUTS] - pl.program_id(0) % CUTS * length
    place = pl.ds(pl.multiple_of(pl.program_id(0) * length, length), length)
    low = jnp.bfloat16

    @pl.when(pl.program_id(0) == 0)
    def _():
        vector_grad_ref[...] = jnp.zeros(vector_grad_ref.shape, jnp.float32)

    joined_ref[place, :ATT] = context_ref[0]
    joined_ref[place, ATT:] = span_ref[0]

    scaling, offsets, stretch, displace = (
        vectors_ref[KERNEL + i : KERNEL + i + 1, :] for i in range(4)
    )
    quarters = (part0_ref, part1_ref, part2_ref, part3_ref)
    tokens = tokens_ref[0]
    valid = row_of(tokens.shape) < count
    value = dot(joined_ref[place, :], second_ref[:, 2 * ATT :])
    value = value + jnp.where(valid, tokens.astype(jnp.float32), 0.0)
    unit_one, scale_one = unit_of(value)
    normed_one = unit_one * scaling + offsets
    normed_ref[place, :] = normed_one.astype(low)
    parts = []
    for g in range(GROUPS):
        lanes = slice(g * WIDE, (g + 1) * WIDE)
        inner = slice(D + g * WIDE, D + (g + 1) * WIDE)
        total = None
        for h in range(4):
            units = slice(h * D // 2, (h + 1) * D // 2)
            hidden = dot_nt(normed_ref[place, lanes], quarters[h][:, inner])
            even = 0.5 * (1.0 + lax.erf(hidden * root_half))
            active = (hidden * even).astype(low)
            active_ref[g, place, units] = active
            slope_ref[g, :, units] = even + hidden * jnp.exp(-0.5 * hidden * hidden) * slope_factor
            part = dot(active, quarters[h][:, lanes])
            total = part if total is None else total + part
        parts.append(total)
    unit_two, scale_two = unit_of(jnp.concatenate(parts, axis=1) + normed_one)
    result = unit_two * stretch + displace
    activations_ref[0] = jnp.where(valid, result, 0.0).astype(low)
    grad = jnp.where(valid, cotangent_ref[0].astype(jnp.float32), 0.0)
    vector_grad_ref[2:3, :] += jnp.sum(grad * unit_two, axis=0, keepdims=True)
    vector_grad_ref[3:4, :] += jnp.sum(grad, axis=0, keepdims=True)
    grad_two = norm_back(grad, unit_two, scale_two, stretch)
    grad_ref[place, :] = grad_two.astype(low)
    parts = []
    for g in range(GROUPS):
        lanes = slice(g * WIDE, (g + 1) * WIDE)
        inner = slice(D + g * WIDE, D + (g + 1) * WIDE)
        total = None
        for h in range(4):
            units = slice(h * D // 2, (h + 1) * D // 2)
            hidden = dot_nt(grad_ref[place, lanes], quarters[h][:, lanes]) * slope_ref[g, :, units]
            hidden = hidden.astype(low)
            hidden_ref[g, place, units] = hidden
            part = dot(hidden, quarters[h][:, inner])
            total = part if total is None else total + part
        parts.append(total)
    grad = grad_two + jnp.concatenate(parts, axis=1)
    vector_grad_ref[0:1, :] += jnp.sum(grad * unit_one, axis=0, keepdims=True)
    vector_grad_ref[1:2, :] += jnp.sum(grad, axis=0, keepdims=True)
    grad = norm_back(grad, unit_one, scale_one, scaling)
    grad_one_ref[0] = grad
    low_grad = grad.astype(low)
    attended_ref[place, :] = low_grad
    grad_context_ref[0] = dot_nt(low_grad, second_ref[:ATT, 2 * ATT :]).astype(low)
    grad_span_ref[0] = dot_nt(low_grad, second_ref[ATT:, 2 * ATT :])

    @pl.when(pl.program_id(0) == pl.num_programs(0) - 1)
    def _():
        for g in range(GROUPS):
            lanes = slice(g * WIDE, (g + 1) * WIDE)
            inner = slice(D + g * WIDE, D + (g + 1) * WIDE)
            for h in range(4):
                units = slice(h * D // 2, (h + 1) * D // 2)
                out = send_ref if h % 2 else keep_ref
                total = dot_tn(active_ref[g, :, units], grad_ref[:, lanes])
                out[h // 2, :, lanes] = total.astype(out.dtype)
                total = dot_tn(hidden_ref[g, :, units], normed_ref[:, lanes])
                out[h // 2, :, inner] = total.astype(out.dtype)
        output_grad_ref[...] = dot_tn(joined_ref[...], attended_ref[...])


def feed_call(lengths, tokens, context, span, cotangent, second, quarters, vectors):
    length = tokens.shape[1]
    outs = [(D, LOW), (D, FULL), (ATT, LOW), (ATT, FULL)]
    wholes = [
        ((2, D // 2, 2 * D), LOW), ((2, D // 2, 2 * D), FULL), ((D, D), FULL), ((8, D), FULL),
    ]
    rows = tokens.shape[0] * length
    scratch = [((GROUPS, length // CUTS, 2 * D), FULL)] + [((GROUPS, rows, 2 * D), LOW)] * 2
    scratch += [((rows, D), LOW)] * 4
    return per_sequence(
        feed_kernel, "feed", [lengths], [tokens, context, span, cotangent],
        [second, *quarters, vectors], outs, wholes, scratch, single=True, cuts=CUTS,
    )


def tokens_kernel(
    lengths_ref, query_ref, keys_ref, values_ref, span_ref, one_ref, conv_ref, first_ref,
    second_ref, out_ref,
):
    count = lengths_ref[pl.program_id(0)]
    total = one_ref[0] + conv_ref[0]
    total = total + dot_nt(query_ref[0], first_ref[:, :ATT])
    total = total + dot_nt(keys_ref[0], first_ref[:, ATT : 2 * ATT])
    total = total + dot_nt(values_ref[0], second_ref[:, :ATT])
    total = total + dot_nt(span_ref[0], second_ref[:, ATT : 2 * ATT])
    out_ref[0] = jnp.where(row_of(total.shape) < count, total, 0.0)


def tokens_call(lengths, grads, first, second):
    return per_sequence(
        tokens_kernel, "tokens_grad", [lengths], grads, [first, second], [(D, FULL)], [], []
    )[0]


def span_back_kernel(
    grad_span_ref, tapw_ref, span_ref, mixture_ref, query_ref, conv_ref, taps_ref,
    grad_spanv_ref, grad_mixconv_ref, grad_conv_ref, taps_grad_ref,
    span_padded_ref, grad_padded_ref, tapw_padded_ref, logit_ref, spread_ref, gather_ref,
):
    length = span_ref.shape[1]
    low = jnp.bfloat16

    @pl.when(pl.program_id(0) == 0)
    def _():
        fill_spread(spread_ref)
        shape = (ATT, 128)
        for m in range(KERNEL):
            hit = lane_of(shape) == m * SLOTS + row_of(shape) // HEAD
            gather_ref[m] = jnp.where(hit, 1.0, 0.0).astype(low)
        taps_grad_ref[...] = jnp.zeros(taps_grad_ref.shape, jnp.float32)

    inside = slice(HALO, HALO + length)
    for ref in (span_padded_ref, grad_padded_ref, tapw_padded_ref):
        pad_rows(ref, length)
    span_padded_ref[inside, :] = span_ref[0]
    grad_padded_ref[inside, :] = grad_span_ref[0]
    tapw_padded_ref[inside, :] = tapw_ref[0]

    def span_chunk(i, carry):
        start = pl.multiple_of(i * CHUNK, CHUNK)
        place = pl.ds(start, CHUNK)
        around = pl.ds(start, CHUNK + 2 * HALO)
        spans = span_padded_ref[around, :]
        grads = grad_padded_ref[around, :]
        both = high_low(tapw_padded_ref[around, :])
        own = grads[HALO : HALO + CHUNK]
        grad_taps = None
        total = None
        for m in range(KERNEL):
            product = shifted(spans, HALO - KERNEL // 2 + m, CHUNK) * own
            part = dot(product.astype(low), gather_ref[m])
            grad_taps = part if grad_taps is None else grad_taps + part
            spread = dot(both, spread_ref[m]) * grads
            term = shifted(spread, HALO + KERNEL // 2 - m, CHUNK)
            total = term if total is None else total + term
        grad_spanv_ref[0, place, :] = total.astype(low)
        weights = tapw_ref[0, place, :]
        centre = over_taps(weights * grad_taps, jnp.add)
        logit_ref[place, :] = (weights * (grad_taps - centre)).astype(low)
        return carry

    lax.fori_loop(0, length // CHUNK, span_chunk, 0)
    grad_logits = logit_ref[...]
    taps_grad_ref[...] += dot_tn(mixture_ref[0], grad_logits)
    grad_mixture = dot_nt(grad_logits, taps_ref[...])
    grad_conv_ref[0] = (grad_mixture * query_ref[0].astype(jnp.float32)).astype(low)
    grad_mixconv_ref[0] = grad_mixture * conv_ref[0]


def span_back_call(grad_span, tapw, span, mixture, query, conv, taps):
    length = span.shape[1]
    rows = length + 2 * HALO
    return per_sequence(
        span_back_kernel, "span_back", [],
        [grad_span, tapw, span, mixture, query, conv], [taps],
        [(ATT, LOW), (ATT, FULL), (ATT, LOW)], [((ATT, 128), FULL)],
        [
            ((rows, ATT), FULL), ((rows, ATT), FULL), ((rows, 128), FULL), ((length, 128), LOW),
            ((KERNEL, 256, ATT), LOW), ((KERNEL, ATT, 128), LOW),
        ],
    )


def depth_back_kernel(
    lengths_ref, tokens_ref, grad_conv_ref, depthwise_ref, first_ref, vectors_ref, taps_grad_ref,
    vector_grad_ref,
    grad_tokens_ref, point_grad_ref, small_ref, padded_ref, back_padded_ref, sums_ref,
):
    length = tokens_ref.shape[1]
    count = lengths_ref[pl.program_id(0)]
    low = jnp.bfloat16

    @pl.when(pl.program_id(0) == 0)
    def _():
        point_grad_ref[...] = jnp.zeros(point_grad_ref.shape, jnp.float32)
        sums_ref[...] = jnp.zeros(sums_ref.shape, jnp.float32)

    inside = slice(HALO, HALO + length)
    for ref in (padded_ref, back_padded_ref):
        pad_rows(ref, length)
    tokens = tokens_ref[0]
    padded_ref[inside, :] = jnp.where(row_of(tokens.shape) < count, tokens.astype(jnp.float32), 0.0)
    point_grad_ref[...] += dot_tn(depthwise_ref[0], grad_conv_ref[0])
    back_padded_ref[inside, :] = dot_nt(grad_conv_ref[0], first_ref[:, 2 * ATT : 3 * ATT])

    def depth_chunk(i, carry):
        start = pl.multiple_of(i * CHUNK, CHUNK)
        around = pl.ds(start, CHUNK + 2 * HALO)
        tokens = padded_ref[around, :]
        grads = back_padded_ref[around, :]
        own = grads[HALO : HALO + CHUNK]
        total = None
        for m in range(KERNEL):
            product = shifted(tokens, HALO - KERNEL // 2 + m, CHUNK) * own
            part = product[0:8]
            for r in range(8, CHUNK, 8):
                part = part + product[r : r + 8]
            sums_ref[m * 8 : m * 8 + 8, :] += part
            term = shifted(grads, HALO + KERNEL // 2 - m, CHUNK) * vectors_ref[m : m + 1, :]
            total = term if total is None else total + term
        grad_tokens_ref[0, pl.ds(start, CHUNK), :] = total
        return carry

    lax.fori_loop(0, length // CHUNK, depth_chunk, 0)

    @pl.when(pl.program_id(0) == pl.num_programs(0) - 1)
    def _():
        depth_grad = [
            jnp.sum(sums_ref[m * 8 : m * 8 + 8, :], axis=0, keepdims=True) for m in range(KERNEL)
        ]
        vector_grad = [vector_grad_ref[i : i + 1, :] for i in range(4)]
        filler = [jnp.zeros((128 - KERNEL - 4, D), jnp.float32)]
        total = jnp.concatenate(depth_grad + vector_grad + filler, axis=0).T
        rows, lanes = small_turns()
        grad = taps_grad_ref[...]
        high = grad.astype(low)
        rest = (grad - high.astype(jnp.float32)).astype(low)
        for b in range(2):
            for part in (high, rest):
                moved = dot_nt(part, lanes[b]).astype(low)
                total = total + dot_tn(rows[b], moved)
        small_ref[...] = total


def depth_back_call(lengths, tokens, grad_conv, depthwise, first, vectors, taps_grad, vector_grad):
    rows = tokens.shape[1] + 2 * HALO
    return per_sequence(
        depth_back_kernel, "depth_back", [lengths], [tokens, grad_conv, depthwise],
        [first, vectors, taps_grad, vector_grad], [(D, FULL)],
        [((D, ATT), FULL), ((D, 128), FULL)],
        [((rows, D), FULL), ((rows, D), FULL), ((KERNEL * 8, D), FULL)],
    )


def attend_back_kernel(
    index, lengths_ref, query_ref, keys_ref, values_ref, logsum_ref, grad_context_ref,
    mixconv_ref, *refs,
):
    grad_query_ref, grad_keys_ref, grad_values_ref = refs[-6:-3]
    turned_ref, keys_sum_ref, values_sum_ref = refs[-3:]
    length = query_ref.shape[1]
    count = lengths_ref[index]
    low = jnp.bfloat16
    factor = HEAD ** (-0.5)
    turned_ref[...] = logsum_ref[0].T
    keys_sum_ref[...] = jnp.zeros(keys_sum_ref.shape, jnp.float32)
    values_sum_ref[...] = jnp.zeros(values_sum_ref.shape, jnp.float32)
    part = 256

    for pair in range(HEADS // 2):
        lanes = slice(pair * 128, pair * 128 + 128)

        def chunk(i, carry, pair=pair, lanes=lanes):
            place = pl.ds(pl.multiple_of(i * part, part), part)
            keys = keys_ref[0, :, lanes]
            values = values_ref[0, :, lanes]
            query = query_ref[0, place, lanes].astype(jnp.float32)
            grads = grad_context_ref[0, place, lanes].astype(jnp.float32)
            total = mixconv_ref[0, place, lanes]
            for j in range(2):
                own = lane_of((part, 128)) // HEAD == j
                query_j = jnp.where(own, query, 0.0).astype(low)
                grads_j = jnp.where(own, grads, 0.0).astype(low)
                scores = dot_nt(keys, query_j) * factor
                attention = jnp.exp(scores - turned_ref[pair * 2 + j : pair * 2 + j + 1, place])
                attention = jnp.where(row_of(scores.shape) < count, attention, 0.0)
                grad_attention = dot_nt(values, grads_j)
                values_sum_ref[:, lanes] += dot(attention.astype(low), grads_j)
                centre = jnp.sum(attention * grad_attention, axis=0, keepdims=True)
                grad_scores = (attention * (grad_attention - centre)).astype(low)
                keys_sum_ref[:, lanes] += dot(grad_scores, query_j)
                both = dot_tn(grad_scores, keys)
                total = total + jnp.where(own, both, 0.0) * factor
            grad_query_ref[0, place, lanes] = total.astype(low)
            return carry

        lax.fori_loop(0, length // part, chunk, 0)
    grad_keys_ref[0] = (keys_sum_ref[...] * factor).astype(low)
    grad_values_ref[0] = values_sum_ref[...].astype(low)


def attend_back_call(index, lengths, arrays, filled):
    length = arrays[0].shape[1]
    return one_sequence(
        attend_back_kernel, "attend_back", index, [lengths], arrays, [(ATT, LOW)] * 3,
        [((128, length), FULL), ((length, ATT), FULL), ((length, ATT), FULL)], filled,
    )


class Links:
    def __init__(self, dp, fsdp):
        self.sizes = {"dp": dp, "fsdp": fsdp}
        self.outer = [("dp", 1 << i) for i in range(32) if (1 << i) < dp][::-1]
        inner = [("fsdp", 1 << i) for i in range(1, 32) if (1 << i) < fsdp]
        core = [("fsdp", 1)] if fsdp > 1 else []
        self.tails = (inner + core, inner[::-1] + core)
        self.count = dp * fsdp
        self.named = self.outer + [("fsdp", 1 << i) for i in range(32) if (1 << i) < fsdp][::-1]

    def weight(self, stage):
        axis, bit = stage
        return bit * self.sizes["fsdp"] if axis == "dp" else bit

    def swap(self, value, stage):
        axis, bit = stage
        return lax.ppermute(value, axis, [(i, i ^ bit) for i in range(self.sizes[axis])])

    def slots_of_owners(self, order):
        me = lax.axis_index("dp") * self.sizes["fsdp"] + lax.axis_index("fsdp")
        rel = jnp.arange(self.count, dtype=jnp.int32) ^ me
        slot = jnp.zeros_like(rel)
        for k, stage in enumerate(self.outer + self.tails[order]):
            slot = slot + jnp.where((rel & self.weight(stage)) != 0, 1 << k, 0)
        return slot

    def owners(self, slots, order):
        taken = jnp.take(slots, self.slots_of_owners(order), axis=0, mode="clip")
        return taken.reshape(-1, slots.shape[-1])

    def gather_outer(self, shards):
        blocks = jnp.concatenate(shards, axis=1)[None]
        for stage in self.outer:
            blocks = yield jnp.concatenate([blocks, self.swap(blocks, stage)], axis=0)
        parts, start = [], 0
        for shard in shards:
            parts.append(blocks[..., start : start + shard.shape[1]])
            start += shard.shape[1]
        yield parts

    def gather_tails(self, parts):
        for stages in zip(*self.tails):
            parts = [jnp.concatenate(part, axis=0) for part in parts]
            parts = [[part, self.swap(part, stage)] for part, stage in zip(parts, stages)]
            parts = yield parts

    def reduce_slots(self, send, keep):
        stages = [list(pair) for pair in zip(*self.tails)][::-1] + [[s, s] for s in self.outer[::-1]]
        for k, pair in enumerate(stages):
            if k > 0:
                half = keep.shape[1] // 2
                send, keep = keep[:, half:].astype(jnp.bfloat16), keep[:, :half]
            if pair[0] == pair[1]:
                got = self.swap(send, pair[0])
            else:
                got = jnp.stack([self.swap(send[i], pair[i]) for i in range(2)])
            keep = yield keep + got.astype(jnp.float32)

    def split(self, terms, left, stage):
        axis, bit = stage
        dim = left.index(stage)
        mine = (lax.axis_index(axis) // bit) & 1
        send = [
            lax.dynamic_index_in_dim(t, 1 - mine, dim, keepdims=False).astype(jnp.bfloat16)
            for t in terms
        ]
        keep = [lax.dynamic_index_in_dim(t, mine, dim, keepdims=False) for t in terms]
        return jnp.concatenate(send, axis=-1), jnp.concatenate(keep, axis=-1)

    def reduce_owners(self, first, second):
        lists = [
            [t.reshape((2,) * len(self.named) + (-1, t.shape[-1])) for t in terms]
            for terms in (first, second)
        ]
        lefts = [list(self.named), list(self.named)]
        for pair in [list(pair) for pair in zip(*self.tails)][::-1]:
            halves = [self.split(lists[i], lefts[i], pair[i]) for i in range(2)]
            if pair[0] == pair[1]:
                cut = halves[0][0].shape[-1]
                got = self.swap(jnp.concatenate([halves[0][0], halves[1][0]], axis=-1), pair[0])
                got = [got[..., :cut], got[..., cut:]]
            else:
                got = [self.swap(halves[i][0], pair[i]) for i in range(2)]
            for i in range(2):
                lists[i] = [halves[i][1] + got[i].astype(jnp.float32)]
                lefts[i].remove(pair[i])
            lists = yield lists
        total, left = [lists[0][0], lists[1][0]], lefts[0]
        for stage in self.outer[::-1]:
            send, keep = self.split(total, left, stage)
            total = [keep + self.swap(send, stage).astype(jnp.float32)]
            left.remove(stage)
            total = yield total


class Staged:
    def __init__(self, stages):
        self.stages = stages
        self.value = next(stages)
        self.ended = False

    def behind(self, value):
        value = self.meet(value)
        self.step()
        return value

    def meet(self, value):
        if not self.ended:
            value, self.value = lax.optimization_barrier((value, self.value))
        return value

    def step(self):
        if not self.ended:
            try:
                self.value = self.stages.send(self.value)
            except StopIteration:
                self.ended = True

    def finish(self):
        while not self.ended:
            self.step()
        return self.value


def on_device(
    links,
    tokens,
    lengths,
    query_weight,
    key_weight,
    value_weight,
    depth_weight,
    point_weight,
    taps_weight,
    span_weight,
    output_weight,
    scaling,
    offsets,
    inner_weight,
    outer_weight,
    stretch,
    displace,
    cotangent,
):
    rows = query_weight.shape[0]
    packed = jnp.concatenate(
        [
            depth_weight.T,
            scaling[:, None],
            offsets[:, None],
            stretch[:, None],
            displace[:, None],
            taps_weight.reshape(rows, -1),
        ],
        axis=1,
    )
    used = packed.shape[1]
    packed = jnp.pad(packed, ((0, 0), (0, 128 - used)))
    grouped = jnp.concatenate(
        [outer_weight[0], outer_weight[1], inner_weight[0].T, inner_weight[1].T], axis=1
    )
    parts = Staged(
        links.gather_outer(
            [
                jnp.concatenate([query_weight, key_weight, point_weight, packed], axis=1),
                jnp.concatenate([value_weight, span_weight, output_weight], axis=1),
            ]
        )
    ).finish()
    parts, grouped = lax.optimization_barrier((parts, grouped))
    leading = Staged(links.gather_tails([[part] for part in parts]))
    outer = Staged(links.gather_outer([grouped[:rows], grouped[rows:]]))
    while not leading.ended:
        outer.value = leading.behind(outer.value)
        outer.step()
    slots = leading.finish()
    first, second = (links.owners(jnp.concatenate(slots[i], axis=0), i) for i in range(2))
    first, second, parts = lax.optimization_barrier((first, second, outer.finish()))
    gathering = Staged(links.gather_tails([[part] for part in parts]))

    (
        query, keys, values, key_conv, depthwise, mixture, tap_weights, span_values, vectors, taps,
    ) = project_call(lengths, tokens, first, second)
    query = gathering.behind(query)
    context, logsum = attend_call(lengths, query, keys, values)
    tap_weights, context = gathering.behind((tap_weights, context))
    span_output = span_call(tap_weights, span_values)
    span_output = gathering.behind(span_output)
    quarters = [piece.reshape(D // 2, 2 * D) for half in gathering.finish() for piece in half]

    (
        activations, grad_one, grad_context, grad_span, send, keep, output_grad, vector_grad,
    ) = feed_call(lengths, tokens, context, span_output, cotangent, second, quarters, vectors)
    reducing = Staged(links.reduce_slots(send, keep))
    grad_span_values, grad_mixconv, grad_conv, taps_grad = span_back_call(
        grad_span, tap_weights, span_values, mixture, query, key_conv, taps
    )
    grad_conv = reducing.behind(grad_conv)
    grad_shifted, point_grad, small_grad = depth_back_call(
        lengths, tokens, grad_conv, depthwise, first, vectors, taps_grad, vector_grad
    )
    grad_mixconv, grad_shifted = reducing.behind((grad_mixconv, grad_shifted))
    grads = []
    for index in range(tokens.shape[0]):
        arrays = [query, keys, values, logsum, grad_context, grad_mixconv]
        grads = attend_back_call(index, lengths, arrays, grads)
        grads = reducing.behind(grads)
    grad_query, grad_keys, grad_values = grads
    positions = lax.broadcasted_iota(jnp.int32, tokens.shape[:2], 1)
    masked = tokens * (positions < lengths[:, None]).astype(tokens.dtype)[..., None]
    qk_grad = weight_term(masked, jnp.concatenate([grad_query, grad_keys], axis=-1))
    vs_grad = weight_term(masked, jnp.concatenate([grad_values, grad_span_values], axis=-1))
    summing = Staged(links.reduce_owners([qk_grad, point_grad, small_grad], [vs_grad, output_grad]))
    grad_one = summing.behind(grad_one)
    tokens_grad = tokens_call(
        lengths,
        [grad_query, grad_keys, grad_values, grad_span_values, grad_one, grad_shifted],
        first,
        second,
    )
    tokens_grad = reducing.meet(tokens_grad)
    tokens_grad = summing.meet(tokens_grad)
    grouped_sum = reducing.finish().reshape(-1, 2 * D)
    summed = summing.finish()[0]
    wide = WIDE
    small_sum = summed[:, 3 * ATT : 3 * ATT + 128]
    second_sum = summed[:, 3 * ATT + 128 :]
    return (
        activations,
        tokens_grad,
        summed[:, :ATT],
        summed[:, ATT : 2 * ATT],
        second_sum[:, :ATT],
        small_sum[:, :KERNEL].T,
        summed[:, 2 * ATT : 3 * ATT],
        small_sum[:, KERNEL + 4 : used].reshape(-1),
        second_sum[:, ATT : 2 * ATT],
        second_sum[:, 2 * ATT :],
        small_sum[:, KERNEL],
        small_sum[:, KERNEL + 1],
        jnp.stack([grouped_sum[:, D + g * wide : D + (g + 1) * wide].T for g in range(GROUPS)]),
        jnp.stack([grouped_sum[:, g * wide : (g + 1) * wide] for g in range(GROUPS)]),
        small_sum[:, KERNEL + 2],
        small_sum[:, KERNEL + 3],
    )


def solution(mesh):
    both = ("dp", "fsdp")
    weights = (
        P(both, None),
        P(both, None),
        P(both, None),
        P(None, both),
        P(both, None),
        P(both),
        P(both, None),
        P(both, None),
        P(both),
        P(both),
        P(None, None, both),
        P(None, both, None),
        P(both),
        P(both),
    )
    row = P(both, None, None)
    links = Links(mesh.shape["dp"], mesh.shape["fsdp"])

    def body(*args):
        return on_device(links, *args)

    return jax.shard_map(
        body,
        mesh=mesh,
        in_specs=(row, P(both)) + weights + (row,),
        out_specs=(row, row) + weights,
        check_vma=False,
    )
```

```python
import functools

import jax
import jax.numpy as jnp
from jax import lax
from jax.experimental import pallas as pl
from jax.experimental.pallas import tpu as pltpu
from jax.sharding import PartitionSpec as P

D = 768
HEADS = 6
HEAD = 64
KERNEL = 9
GROUPS = 2
ATT = 384

epsilon = 1e-06
masked_score = -1000000000.0
root_half = 0.7071067811865476
slope_factor = 0.3989422804014327


def weight_term(left, grad_out):
    return jnp.einsum("bsk,bsn->kn", left, grad_out, preferred_element_type=jnp.float32)


CHUNK = 128
CUTS = 2
HALO = 8
SLOTS = 8
WIDE = D // GROUPS


def dot(a, b):
    return jnp.dot(a, b, preferred_element_type=jnp.float32)


def dot_nt(a, b):
    return lax.dot_general(a, b, (((1,), (1,)), ((), ())), preferred_element_type=jnp.float32)


def dot_tn(a, b):
    return lax.dot_general(a, b, (((0,), (0,)), ((), ())), preferred_element_type=jnp.float32)


def lane_of(shape):
    return lax.broadcasted_iota(jnp.int32, shape, len(shape) - 1)


def row_of(shape):
    return lax.broadcasted_iota(jnp.int32, shape, len(shape) - 2)


def shifted(value, offset, count):
    if offset % 8:
        value = pltpu.roll(value, value.shape[0] - offset, axis=0)
        offset = 0
    return value[offset : offset + count]


def high_low(value):
    high = value.astype(jnp.bfloat16)
    low = (value - high.astype(jnp.float32)).astype(jnp.bfloat16)
    return jnp.concatenate([high, low], axis=1)


def over_taps(value, combine):
    for step in (8, 16, 32, 64):
        value = combine(value, pltpu.roll(value, step, axis=1))
    return value


def fill_spread(spread_ref):
    shape = (256, ATT)
    for m in range(KERNEL):
        lanes = row_of(shape) % 128
        head = lane_of(shape) // HEAD
        spread_ref[m] = jnp.where(lanes == m * SLOTS + head, 1.0, 0.0).astype(jnp.bfloat16)


def pad_rows(ref, length):
    zeros = jnp.zeros((HALO, ref.shape[1]), ref.dtype)
    ref[0:HALO, :] = zeros
    ref[HALO + length : 2 * HALO + length, :] = zeros


def small_turns():
    low = jnp.bfloat16
    rows = [
        jnp.where(lane_of((ATT, D)) == 2 * row_of((ATT, D)) + b, 1.0, 0.0).astype(low)
        for b in range(2)
    ]
    near, far = row_of((128, 128)), lane_of((128, 128))
    tap, head = far // SLOTS, far % SLOTS
    lanes = []
    for b in range(2):
        hit = (near == KERNEL + 4 + (head - 3 * b) * KERNEL + tap) & (tap < KERNEL)
        hit = hit & (head >= 3 * b) & (head < 3 * b + 3)
        lanes.append(jnp.where(hit, 1.0, 0.0).astype(low))
    return rows, lanes


def project_kernel(
    lengths_ref, tokens_ref, first_ref, second_ref,
    query_ref, keys_ref, values_ref, conv_ref, depthwise_ref, mixture_ref, tapw_ref, span_ref,
    vectors_ref, taps_ref, padded_ref,
):
    length = tokens_ref.shape[1]
    count = lengths_ref[pl.program_id(0)]
    low = jnp.bfloat16

    @pl.when(pl.program_id(0) == 0)
    def _():
        small = first_ref[:, 3 * ATT : 3 * ATT + 128]
        vectors_ref[...] = small.astype(jnp.float32).T[:16]
        rows, lanes = small_turns()
        total = None
        for b in range(2):
            part = dot(rows[b], dot(small, lanes[b]).astype(low))
            total = part if total is None else total + part
        taps_ref[...] = total.astype(low)

    pad_rows(padded_ref, length)
    tokens = tokens_ref[0]
    masked = jnp.where(row_of(tokens.shape) < count, tokens.astype(jnp.float32), 0.0)
    padded_ref[HALO : HALO + length, :] = masked
    masked = masked.astype(low)
    query_ref[0] = dot(masked, first_ref[:, :ATT]).astype(low)
    keys_ref[0] = dot(masked, first_ref[:, ATT : 2 * ATT]).astype(low)
    values_ref[0] = dot(masked, second_ref[:, :ATT]).astype(low)
    span_ref[0] = dot(masked, second_ref[:, ATT : 2 * ATT])

    def depth_chunk(i, carry):
        start = pl.multiple_of(i * CHUNK, CHUNK)
        block = padded_ref[pl.ds(start, CHUNK + 2 * HALO), :]
        total = None
        for m in range(KERNEL):
            term = shifted(block, HALO - KERNEL // 2 + m, CHUNK) * vectors_ref[m : m + 1, :]
            total = term if total is None else total + term
        depthwise_ref[0, pl.ds(start, CHUNK), :] = total.astype(low)
        return carry

    lax.fori_loop(0, length // CHUNK, depth_chunk, 0)
    conv = dot(depthwise_ref[0], first_ref[:, 2 * ATT : 3 * ATT])
    conv_ref[0] = conv
    mixture_ref[0] = (conv * query_ref[0].astype(jnp.float32)).astype(low)
    logits = dot(mixture_ref[0], taps_ref[...])
    logits = jnp.where(lane_of(logits.shape) < KERNEL * SLOTS, logits, -1e30)
    exponent = jnp.exp(logits - over_taps(logits, jnp.maximum))
    tapw_ref[0] = exponent / over_taps(exponent, jnp.add)


def span_kernel(tapw_ref, span_ref, out_ref, span_padded_ref, spread_ref):
    length = span_ref.shape[1]

    @pl.when(pl.program_id(0) == 0)
    def _():
        fill_spread(spread_ref)

    pad_rows(span_padded_ref, length)
    span_padded_ref[HALO : HALO + length, :] = span_ref[0]

    def span_chunk(i, carry):
        start = pl.multiple_of(i * CHUNK, CHUNK)
        block = span_padded_ref[pl.ds(start, CHUNK + 2 * HALO), :]
        both = high_low(tapw_ref[0, pl.ds(start, CHUNK), :])
        total = None
        for m in range(KERNEL):
            term = shifted(block, HALO - KERNEL // 2 + m, CHUNK) * dot(both, spread_ref[m])
            total = term if total is None else total + term
        out_ref[0, pl.ds(start, CHUNK), :] = total.astype(jnp.bfloat16)
        return carry

    lax.fori_loop(0, length // CHUNK, span_chunk, 0)


def attend_kernel(lengths_ref, query_ref, keys_ref, values_ref, context_ref, logsum_ref):
    length = query_ref.shape[1]
    count = lengths_ref[pl.program_id(0)]
    low = jnp.bfloat16
    rows = 256

    def attend_pair(index, carry):
        pair, half = index // (length // rows), index % (length // rows)
        lanes = pl.ds(pl.multiple_of(pair * 128, 128), 128)
        place = pl.ds(pl.multiple_of(half * rows, rows), rows)
        query = query_ref[0, place, lanes]
        keys = keys_ref[0, :, lanes]
        values = values_ref[0, :, lanes]
        left = lane_of((rows, 128)) < HEAD
        sums = logsum_ref[0, place, :]
        contexts = []
        for j in range(2):
            mine = left if j == 0 else jnp.logical_not(left)
            own = jnp.where(mine, query.astype(jnp.float32), 0.0).astype(low)
            scores = dot_nt(own, keys) * HEAD ** (-0.5)
            scores = jnp.where(lane_of(scores.shape) < count, scores, masked_score)
            highest = jnp.max(scores, axis=-1, keepdims=True)
            exponent = jnp.exp(scores - highest)
            totals = jnp.sum(exponent, axis=-1, keepdims=True)
            contexts.append(dot((exponent * (1.0 / totals)).astype(low), values))
            sums = jnp.where(lane_of(sums.shape) == pair * 2 + j, highest + jnp.log(totals), sums)
        logsum_ref[0, place, :] = sums
        context_ref[0, place, lanes] = jnp.where(left, contexts[0], contexts[1]).astype(low)
        return carry

    logsum_ref[0] = jnp.zeros(logsum_ref.shape[1:], jnp.float32)
    lax.fori_loop(0, (HEADS // 2) * (length // rows), attend_pair, 0)


def whole_spec(shape, single=False):
    mode = {"pipeline_mode": pl.Buffered(1)} if single else {}
    return pl.BlockSpec(shape, lambda i, *_: (0,) * len(shape), **mode)


def seq_spec(length, width, cuts=1):
    return pl.BlockSpec((1, length // cuts, width), lambda i, *_: (i // cuts, i % cuts, 0))


LIMIT = pltpu.CompilerParams(vmem_limit_bytes=60 * 1024 * 1024, dimension_semantics=("arbitrary",))


def eye_at(shape, start):
    return jnp.where(lane_of(shape) == row_of(shape) + start, 1.0, 0.0).astype(jnp.bfloat16)


def pack_kernel(
    query_ref, key_ref, point_ref, value_ref, span_ref, output_ref, vectors_ref, taps_ref,
    inner_ref, outer_ref, first_ref, second_ref,
):
    low = jnp.bfloat16
    rows = query_ref.shape[0]
    first_ref[:, :ATT] = query_ref[...]
    first_ref[:, ATT : 2 * ATT] = key_ref[...]
    first_ref[:, 2 * ATT : 3 * ATT] = point_ref[...]
    small = dot_tn(vectors_ref[...], eye_at((vectors_ref.shape[0], 128), 0))
    small = small + dot(taps_ref[...], eye_at((taps_ref.shape[1], 128), KERNEL + 4))
    first_ref[:, 3 * ATT : 3 * ATT + 128] = small.astype(low)
    start = 3 * ATT + 128
    first_ref[:, start : start + ATT] = value_ref[...]
    first_ref[:, start + ATT : start + 2 * ATT] = span_ref[...]
    first_ref[:, start + 2 * ATT :] = output_ref[...]
    for g in range(GROUPS):
        outer = outer_ref[g].astype(jnp.float32)
        inner = inner_ref[g].astype(jnp.float32)
        for h in range(2):
            start = h * 2 * D + g * WIDE
            part = slice(h * rows, (h + 1) * rows)
            second_ref[:, start : start + WIDE] = outer[part].astype(low)
            second_ref[:, start + D : start + D + WIDE] = inner[part].astype(low)


def one_sequence(kernel, name, index, scalars, arrays, outs, scratch, filled):
    seqs, length = arrays[0].shape[:2]

    def spec(width):
        return pl.BlockSpec((1, length, width), lambda i, *_: (index, 0, 0))

    inputs = len(scalars) + len(arrays)
    return pl.pallas_call(
        functools.partial(kernel, index),
        grid_spec=pltpu.PrefetchScalarGridSpec(
            num_scalar_prefetch=len(scalars),
            grid=(1,),
            in_specs=[spec(a.shape[2]) for a in arrays]
            + [pl.BlockSpec(memory_space=pl.ANY) for _ in filled],
            out_specs=[spec(w) for w, _ in outs],
            scratch_shapes=[pltpu.VMEM(s, t) for s, t in scratch],
        ),
        out_shape=[jax.ShapeDtypeStruct((seqs, length, w), t) for w, t in outs],
        input_output_aliases={inputs + i: i for i in range(len(filled))},
        compiler_params=LIMIT,
        name=name,
    )(*scalars, *arrays, *filled)


def per_sequence(
    kernel, name, scalars, arrays, weights, outs, wholes, scratch, single=False, cuts=1
):
    seqs, length = arrays[0].shape[:2]
    return pl.pallas_call(
        kernel,
        grid_spec=pltpu.PrefetchScalarGridSpec(
            num_scalar_prefetch=len(scalars),
            grid=(seqs * cuts,),
            in_specs=[seq_spec(length, a.shape[2], cuts) for a in arrays]
            + [whole_spec(a.shape, single) for a in weights],
            out_specs=[seq_spec(length, w, cuts) for w, _ in outs]
            + [whole_spec(s, single) for s, _ in wholes],
            scratch_shapes=[pltpu.VMEM(s, t) for s, t in scratch],
        ),
        out_shape=[jax.ShapeDtypeStruct((seqs, length, w), t) for w, t in outs]
        + [jax.ShapeDtypeStruct(s, t) for s, t in wholes],
        compiler_params=LIMIT,
        name=name,
    )(*scalars, *arrays, *weights)


LOW, FULL = jnp.bfloat16, jnp.float32


def project_call(lengths, tokens, first, second):
    outs = [
        (ATT, LOW), (ATT, LOW), (ATT, LOW), (ATT, FULL), (D, LOW), (ATT, LOW), (128, FULL),
        (ATT, FULL),
    ]
    return per_sequence(
        project_kernel, "project", [lengths], [tokens], [first, second], outs,
        [((16, D), FULL), ((ATT, 128), LOW)], [((tokens.shape[1] + 2 * HALO, D), FULL)],
    )


def span_call(tapw, span):
    scratch = [((span.shape[1] + 2 * HALO, ATT), FULL), ((KERNEL, 256, ATT), LOW)]
    return per_sequence(span_kernel, "span", [], [tapw, span], [], [(ATT, LOW)], [], scratch)[0]


def attend_call(lengths, query, keys, values):
    outs = [(ATT, LOW), (128, FULL)]
    return per_sequence(
        attend_kernel, "attend", [lengths], [query, keys, values], [], outs, [], []
    )


def unit_of(value):
    mean = jnp.mean(value, axis=-1, keepdims=True)
    centered = value - mean
    scale = lax.rsqrt(jnp.mean(centered * centered, axis=-1, keepdims=True) + epsilon)
    return centered * scale, scale


def norm_back(grad_out, unit, scale, gain):
    scaled = grad_out * gain
    return scale * (
        scaled
        - jnp.mean(scaled, axis=-1, keepdims=True)
        - unit * jnp.mean(scaled * unit, axis=-1, keepdims=True)
    )


def feed_kernel(
    lengths_ref, tokens_ref, context_ref, span_ref, cotangent_ref, second_ref, part0_ref,
    part1_ref, part2_ref, part3_ref, vectors_ref,
    activations_ref, grad_one_ref, grad_context_ref, grad_span_ref, send_ref, keep_ref,
    output_grad_ref, vector_grad_ref,
    slope_ref, active_ref, hidden_ref, normed_ref, grad_ref, attended_ref, joined_ref,
):
    length = tokens_ref.shape[1]
    count = lengths_ref[pl.program_id(0) // CUTS] - pl.program_id(0) % CUTS * length
    place = pl.ds(pl.multiple_of(pl.program_id(0) * length, length), length)
    low = jnp.bfloat16

    @pl.when(pl.program_id(0) == 0)
    def _():
        vector_grad_ref[...] = jnp.zeros(vector_grad_ref.shape, jnp.float32)

    joined_ref[place, :ATT] = context_ref[0]
    joined_ref[place, ATT:] = span_ref[0]

    scaling, offsets, stretch, displace = (
        vectors_ref[KERNEL + i : KERNEL + i + 1, :] for i in range(4)
    )
    quarters = (part0_ref, part1_ref, part2_ref, part3_ref)
    tokens = tokens_ref[0]
    valid = row_of(tokens.shape) < count
    value = dot(joined_ref[place, :], second_ref[:, 2 * ATT :])
    value = value + jnp.where(valid, tokens.astype(jnp.float32), 0.0)
    unit_one, scale_one = unit_of(value)
    normed_one = unit_one * scaling + offsets
    normed_ref[place, :] = normed_one.astype(low)
    parts = []
    for g in range(GROUPS):
        lanes = slice(g * WIDE, (g + 1) * WIDE)
        inner = slice(D + g * WIDE, D + (g + 1) * WIDE)
        total = None
        for h in range(4):
            units = slice(h * D // 2, (h + 1) * D // 2)
            hidden = dot_nt(normed_ref[place, lanes], quarters[h][:, inner])
            even = 0.5 * (1.0 + lax.erf(hidden * root_half))
            active = (hidden * even).astype(low)
            active_ref[g, place, units] = active
            slope_ref[g, :, units] = even + hidden * jnp.exp(-0.5 * hidden * hidden) * slope_factor
            part = dot(active, quarters[h][:, lanes])
            total = part if total is None else total + part
        parts.append(total)
    unit_two, scale_two = unit_of(jnp.concatenate(parts, axis=1) + normed_one)
    result = unit_two * stretch + displace
    activations_ref[0] = jnp.where(valid, result, 0.0).astype(low)
    grad = jnp.where(valid, cotangent_ref[0].astype(jnp.float32), 0.0)
    vector_grad_ref[2:3, :] += jnp.sum(grad * unit_two, axis=0, keepdims=True)
    vector_grad_ref[3:4, :] += jnp.sum(grad, axis=0, keepdims=True)
    grad_two = norm_back(grad, unit_two, scale_two, stretch)
    grad_ref[place, :] = grad_two.astype(low)
    parts = []
    for g in range(GROUPS):
        lanes = slice(g * WIDE, (g + 1) * WIDE)
        inner = slice(D + g * WIDE, D + (g + 1) * WIDE)
        total = None
        for h in range(4):
            units = slice(h * D // 2, (h + 1) * D // 2)
            hidden = dot_nt(grad_ref[place, lanes], quarters[h][:, lanes]) * slope_ref[g, :, units]
            hidden = hidden.astype(low)
            hidden_ref[g, place, units] = hidden
            part = dot(hidden, quarters[h][:, inner])
            total = part if total is None else total + part
        parts.append(total)
    grad = grad_two + jnp.concatenate(parts, axis=1)
    vector_grad_ref[0:1, :] += jnp.sum(grad * unit_one, axis=0, keepdims=True)
    vector_grad_ref[1:2, :] += jnp.sum(grad, axis=0, keepdims=True)
    grad = norm_back(grad, unit_one, scale_one, scaling)
    grad_one_ref[0] = grad
    low_grad = grad.astype(low)
    attended_ref[place, :] = low_grad
    grad_context_ref[0] = dot_nt(low_grad, second_ref[:ATT, 2 * ATT :]).astype(low)
    grad_span_ref[0] = dot_nt(low_grad, second_ref[ATT:, 2 * ATT :])

    @pl.when(pl.program_id(0) == pl.num_programs(0) - 1)
    def _():
        def terms(index, carry):
            g, half = index // 2, index % 2
            lanes = pl.ds(pl.multiple_of(g * WIDE, WIDE), WIDE)
            inner = pl.ds(pl.multiple_of(D + g * WIDE, WIDE), WIDE)
            for part, out in enumerate((keep_ref, send_ref)):
                start = pl.multiple_of(half * D + part * (D // 2), D // 2)
                units = pl.ds(start, D // 2)
                total = dot_tn(active_ref[g, :, units], grad_ref[:, lanes])
                out[half, :, lanes] = total.astype(out.dtype)
                total = dot_tn(hidden_ref[g, :, units], normed_ref[:, lanes])
                out[half, :, inner] = total.astype(out.dtype)
            return carry

        lax.fori_loop(0, 2 * GROUPS, terms, 0)
        output_grad_ref[...] = dot_tn(joined_ref[...], attended_ref[...])


def feed_call(lengths, tokens, context, span, cotangent, second, quarters, vectors):
    length = tokens.shape[1]
    outs = [(D, LOW), (D, FULL), (ATT, LOW), (ATT, FULL)]
    wholes = [
        ((2, D // 2, 2 * D), LOW), ((2, D // 2, 2 * D), FULL), ((D, D), FULL), ((8, D), FULL),
    ]
    rows = tokens.shape[0] * length
    scratch = [((GROUPS, length // CUTS, 2 * D), FULL)] + [((GROUPS, rows, 2 * D), LOW)] * 2
    scratch += [((rows, D), LOW)] * 4
    return per_sequence(
        feed_kernel, "feed", [lengths], [tokens, context, span, cotangent],
        [second, *quarters, vectors], outs, wholes, scratch, single=True, cuts=CUTS,
    )


def tokens_kernel(
    lengths_ref, query_ref, keys_ref, values_ref, span_ref, one_ref, conv_ref, first_ref,
    second_ref, out_ref,
):
    count = lengths_ref[pl.program_id(0)]
    total = one_ref[0] + conv_ref[0]
    total = total + dot_nt(query_ref[0], first_ref[:, :ATT])
    total = total + dot_nt(keys_ref[0], first_ref[:, ATT : 2 * ATT])
    total = total + dot_nt(values_ref[0], second_ref[:, :ATT])
    total = total + dot_nt(span_ref[0], second_ref[:, ATT : 2 * ATT])
    out_ref[0] = jnp.where(row_of(total.shape) < count, total, 0.0)


def tokens_call(lengths, grads, first, second):
    return per_sequence(
        tokens_kernel, "tokens_grad", [lengths], grads, [first, second], [(D, FULL)], [], []
    )[0]


def span_back_kernel(
    grad_span_ref, tapw_ref, span_ref, mixture_ref, query_ref, conv_ref, taps_ref,
    grad_spanv_ref, grad_mixconv_ref, grad_conv_ref, taps_grad_ref,
    span_padded_ref, grad_padded_ref, tapw_padded_ref, logit_ref, spread_ref, gather_ref,
):
    length = span_ref.shape[1]
    low = jnp.bfloat16

    @pl.when(pl.program_id(0) == 0)
    def _():
        fill_spread(spread_ref)
        shape = (ATT, 128)
        for m in range(KERNEL):
            hit = lane_of(shape) == m * SLOTS + row_of(shape) // HEAD
            gather_ref[m] = jnp.where(hit, 1.0, 0.0).astype(low)
        taps_grad_ref[...] = jnp.zeros(taps_grad_ref.shape, jnp.float32)

    inside = slice(HALO, HALO + length)
    for ref in (span_padded_ref, grad_padded_ref, tapw_padded_ref):
        pad_rows(ref, length)
    span_padded_ref[inside, :] = span_ref[0]
    grad_padded_ref[inside, :] = grad_span_ref[0]
    tapw_padded_ref[inside, :] = tapw_ref[0]

    def span_chunk(i, carry):
        start = pl.multiple_of(i * CHUNK, CHUNK)
        place = pl.ds(start, CHUNK)
        around = pl.ds(start, CHUNK + 2 * HALO)
        spans = span_padded_ref[around, :]
        grads = grad_padded_ref[around, :]
        both = high_low(tapw_padded_ref[around, :])
        own = grads[HALO : HALO + CHUNK]
        grad_taps = None
        total = None
        for m in range(KERNEL):
            product = shifted(spans, HALO - KERNEL // 2 + m, CHUNK) * own
            part = dot(product.astype(low), gather_ref[m])
            grad_taps = part if grad_taps is None else grad_taps + part
            spread = dot(both, spread_ref[m]) * grads
            term = shifted(spread, HALO + KERNEL // 2 - m, CHUNK)
            total = term if total is None else total + term
        grad_spanv_ref[0, place, :] = total.astype(low)
        weights = tapw_ref[0, place, :]
        centre = over_taps(weights * grad_taps, jnp.add)
        logit_ref[place, :] = (weights * (grad_taps - centre)).astype(low)
        return carry

    lax.fori_loop(0, length // CHUNK, span_chunk, 0)
    grad_logits = logit_ref[...]
    taps_grad_ref[...] += dot_tn(mixture_ref[0], grad_logits)
    grad_mixture = dot_nt(grad_logits, taps_ref[...])
    grad_conv_ref[0] = (grad_mixture * query_ref[0].astype(jnp.float32)).astype(low)
    grad_mixconv_ref[0] = grad_mixture * conv_ref[0]


def span_back_call(grad_span, tapw, span, mixture, query, conv, taps):
    length = span.shape[1]
    rows = length + 2 * HALO
    return per_sequence(
        span_back_kernel, "span_back", [],
        [grad_span, tapw, span, mixture, query, conv], [taps],
        [(ATT, LOW), (ATT, FULL), (ATT, LOW)], [((ATT, 128), FULL)],
        [
            ((rows, ATT), FULL), ((rows, ATT), FULL), ((rows, 128), FULL), ((length, 128), LOW),
            ((KERNEL, 256, ATT), LOW), ((KERNEL, ATT, 128), LOW),
        ],
    )


def depth_back_kernel(
    lengths_ref, tokens_ref, grad_conv_ref, depthwise_ref, first_ref, vectors_ref, taps_grad_ref,
    vector_grad_ref,
    grad_tokens_ref, point_grad_ref, small_ref, padded_ref, back_padded_ref, sums_ref,
):
    length = tokens_ref.shape[1]
    count = lengths_ref[pl.program_id(0)]
    low = jnp.bfloat16

    @pl.when(pl.program_id(0) == 0)
    def _():
        point_grad_ref[...] = jnp.zeros(point_grad_ref.shape, jnp.float32)
        sums_ref[...] = jnp.zeros(sums_ref.shape, jnp.float32)

    inside = slice(HALO, HALO + length)
    for ref in (padded_ref, back_padded_ref):
        pad_rows(ref, length)
    tokens = tokens_ref[0]
    padded_ref[inside, :] = jnp.where(row_of(tokens.shape) < count, tokens.astype(jnp.float32), 0.0)
    point_grad_ref[...] += dot_tn(depthwise_ref[0], grad_conv_ref[0])
    back_padded_ref[inside, :] = dot_nt(grad_conv_ref[0], first_ref[:, 2 * ATT : 3 * ATT])

    def depth_chunk(i, carry):
        start = pl.multiple_of(i * CHUNK, CHUNK)
        around = pl.ds(start, CHUNK + 2 * HALO)
        tokens = padded_ref[around, :]
        grads = back_padded_ref[around, :]
        own = grads[HALO : HALO + CHUNK]
        total = None
        for m in range(KERNEL):
            product = shifted(tokens, HALO - KERNEL // 2 + m, CHUNK) * own
            part = product[0:8]
            for r in range(8, CHUNK, 8):
                part = part + product[r : r + 8]
            sums_ref[m * 8 : m * 8 + 8, :] += part
            term = shifted(grads, HALO + KERNEL // 2 - m, CHUNK) * vectors_ref[m : m + 1, :]
            total = term if total is None else total + term
        grad_tokens_ref[0, pl.ds(start, CHUNK), :] = total
        return carry

    lax.fori_loop(0, length // CHUNK, depth_chunk, 0)

    @pl.when(pl.program_id(0) == pl.num_programs(0) - 1)
    def _():
        depth_grad = [
            jnp.sum(sums_ref[m * 8 : m * 8 + 8, :], axis=0, keepdims=True) for m in range(KERNEL)
        ]
        vector_grad = [vector_grad_ref[i : i + 1, :] for i in range(4)]
        filler = [jnp.zeros((128 - KERNEL - 4, D), jnp.float32)]
        total = jnp.concatenate(depth_grad + vector_grad + filler, axis=0).T
        rows, lanes = small_turns()
        grad = taps_grad_ref[...]
        high = grad.astype(low)
        rest = (grad - high.astype(jnp.float32)).astype(low)
        for b in range(2):
            for part in (high, rest):
                moved = dot_nt(part, lanes[b]).astype(low)
                total = total + dot_tn(rows[b], moved)
        small_ref[...] = total


def depth_back_call(lengths, tokens, grad_conv, depthwise, first, vectors, taps_grad, vector_grad):
    rows = tokens.shape[1] + 2 * HALO
    return per_sequence(
        depth_back_kernel, "depth_back", [lengths], [tokens, grad_conv, depthwise],
        [first, vectors, taps_grad, vector_grad], [(D, FULL)],
        [((D, ATT), FULL), ((D, 128), FULL)],
        [((rows, D), FULL), ((rows, D), FULL), ((KERNEL * 8, D), FULL)],
    )


def attend_back_kernel(
    index, lengths_ref, query_ref, keys_ref, values_ref, logsum_ref, grad_context_ref,
    mixconv_ref, *refs,
):
    grad_query_ref, grad_keys_ref, grad_values_ref = refs[-6:-3]
    turned_ref, keys_sum_ref, values_sum_ref = refs[-3:]
    length = query_ref.shape[1]
    count = lengths_ref[index]
    low = jnp.bfloat16
    factor = HEAD ** (-0.5)
    turned_ref[...] = logsum_ref[0].T
    keys_sum_ref[...] = jnp.zeros(keys_sum_ref.shape, jnp.float32)
    values_sum_ref[...] = jnp.zeros(values_sum_ref.shape, jnp.float32)
    part = 256

    def chunk(step, carry):
        pair, i = step // (length // part), step % (length // part)
        lanes = pl.ds(pl.multiple_of(pair * 128, 128), 128)
        place = pl.ds(pl.multiple_of(i * part, part), part)
        keys = keys_ref[0, :, lanes]
        values = values_ref[0, :, lanes]
        query = query_ref[0, place, lanes].astype(jnp.float32)
        grads = grad_context_ref[0, place, lanes].astype(jnp.float32)
        total = mixconv_ref[0, place, lanes]
        for j in range(2):
            own = lane_of((part, 128)) // HEAD == j
            query_j = jnp.where(own, query, 0.0).astype(low)
            grads_j = jnp.where(own, grads, 0.0).astype(low)
            scores = dot_nt(keys, query_j) * factor
            attention = jnp.exp(scores - turned_ref[pl.ds(pair * 2 + j, 1), place])
            attention = jnp.where(row_of(scores.shape) < count, attention, 0.0)
            grad_attention = dot_nt(values, grads_j)
            values_sum_ref[:, lanes] += dot(attention.astype(low), grads_j)
            centre = jnp.sum(attention * grad_attention, axis=0, keepdims=True)
            grad_scores = (attention * (grad_attention - centre)).astype(low)
            keys_sum_ref[:, lanes] += dot(grad_scores, query_j)
            both = dot_tn(grad_scores, keys)
            total = total + jnp.where(own, both, 0.0) * factor
        grad_query_ref[0, place, lanes] = total.astype(low)
        return carry

    lax.fori_loop(0, (HEADS // 2) * (length // part), chunk, 0)
    grad_keys_ref[0] = (keys_sum_ref[...] * factor).astype(low)
    grad_values_ref[0] = values_sum_ref[...].astype(low)


def attend_back_call(index, lengths, arrays, filled):
    length = arrays[0].shape[1]
    return one_sequence(
        attend_back_kernel, "attend_back", index, [lengths], arrays, [(ATT, LOW)] * 3,
        [((128, length), FULL), ((length, ATT), FULL), ((length, ATT), FULL)], filled,
    )


class Links:
    def __init__(self, dp, fsdp):
        self.sizes = {"dp": dp, "fsdp": fsdp}
        self.outer = [("dp", 1 << i) for i in range(32) if (1 << i) < dp][::-1]
        inner = [("fsdp", 1 << i) for i in range(1, 32) if (1 << i) < fsdp]
        core = [("fsdp", 1)] if fsdp > 1 else []
        self.tails = (inner + core, inner[::-1] + core)
        self.count = dp * fsdp
        self.named = self.outer + [("fsdp", 1 << i) for i in range(32) if (1 << i) < fsdp][::-1]

    def weight(self, stage):
        axis, bit = stage
        return bit * self.sizes["fsdp"] if axis == "dp" else bit

    def swap(self, value, stage):
        axis, bit = stage
        return lax.ppermute(value, axis, [(i, i ^ bit) for i in range(self.sizes[axis])])

    def slots_of_owners(self, order):
        me = lax.axis_index("dp") * self.sizes["fsdp"] + lax.axis_index("fsdp")
        rel = jnp.arange(self.count, dtype=jnp.int32) ^ me
        slot = jnp.zeros_like(rel)
        for k, stage in enumerate(self.outer + self.tails[order]):
            slot = slot + jnp.where((rel & self.weight(stage)) != 0, 1 << k, 0)
        return slot

    def owners(self, slots, order):
        taken = jnp.take(slots, self.slots_of_owners(order), axis=0, mode="clip")
        return taken.reshape(-1, slots.shape[-1])

    def gather_outer(self, shard, widths):
        blocks = shard[None]
        for stage in self.outer:
            blocks = yield jnp.concatenate([blocks, self.swap(blocks, stage)], axis=0)
        parts, start = [], 0
        for width in widths:
            parts.append(blocks[..., start : start + width])
            start += width
        yield parts

    def gather_tails(self, parts):
        for stages in zip(*self.tails):
            parts = [jnp.concatenate(part, axis=0) for part in parts]
            parts = [[part, self.swap(part, stage)] for part, stage in zip(parts, stages)]
            parts = yield parts

    def reduce_slots(self, send, keep):
        stages = [list(pair) for pair in zip(*self.tails)][::-1] + [[s, s] for s in self.outer[::-1]]
        for k, pair in enumerate(stages):
            if k > 0:
                half = keep.shape[1] // 2
                send, keep = keep[:, half:].astype(jnp.bfloat16), keep[:, :half]
            if pair[0] == pair[1]:
                got = self.swap(send, pair[0])
            else:
                got = jnp.stack([self.swap(send[i], pair[i]) for i in range(2)])
            keep = yield keep + got.astype(jnp.float32)

    def split(self, terms, left, stage):
        axis, bit = stage
        dim = left.index(stage)
        mine = (lax.axis_index(axis) // bit) & 1
        send = [
            lax.dynamic_index_in_dim(t, 1 - mine, dim, keepdims=False).astype(jnp.bfloat16)
            for t in terms
        ]
        keep = [lax.dynamic_index_in_dim(t, mine, dim, keepdims=False) for t in terms]
        return jnp.concatenate(send, axis=-1), jnp.concatenate(keep, axis=-1)

    def reduce_owners(self, first, second):
        lists = [
            [t.reshape((2,) * len(self.named) + (-1, t.shape[-1])) for t in terms]
            for terms in (first, second)
        ]
        lefts = [list(self.named), list(self.named)]
        for pair in [list(pair) for pair in zip(*self.tails)][::-1]:
            halves = [self.split(lists[i], lefts[i], pair[i]) for i in range(2)]
            if pair[0] == pair[1]:
                cut = halves[0][0].shape[-1]
                got = self.swap(jnp.concatenate([halves[0][0], halves[1][0]], axis=-1), pair[0])
                got = [got[..., :cut], got[..., cut:]]
            else:
                got = [self.swap(halves[i][0], pair[i]) for i in range(2)]
            for i in range(2):
                lists[i] = [halves[i][1] + got[i].astype(jnp.float32)]
                lefts[i].remove(pair[i])
            lists = yield lists
        total, left = [lists[0][0], lists[1][0]], lefts[0]
        for stage in self.outer[::-1]:
            send, keep = self.split(total, left, stage)
            total = [keep + self.swap(send, stage).astype(jnp.float32)]
            left.remove(stage)
            total = yield total


class Staged:
    def __init__(self, stages):
        self.stages = stages
        self.value = next(stages)
        self.ended = False

    def behind(self, value):
        value = self.meet(value)
        self.step()
        return value

    def meet(self, value):
        if not self.ended:
            value, self.value = lax.optimization_barrier((value, self.value))
        return value

    def step(self):
        if not self.ended:
            try:
                self.value = self.stages.send(self.value)
            except StopIteration:
                self.ended = True

    def finish(self):
        while not self.ended:
            self.step()
        return self.value


def on_device(
    links,
    tokens,
    lengths,
    query_weight,
    key_weight,
    value_weight,
    depth_weight,
    point_weight,
    taps_weight,
    span_weight,
    output_weight,
    scaling,
    offsets,
    inner_weight,
    outer_weight,
    stretch,
    displace,
    cotangent,
):
    rows = query_weight.shape[0]
    used = KERNEL + 4 + taps_weight.shape[0] // rows
    vectors = jnp.concatenate(
        [depth_weight, jnp.stack([scaling, offsets, stretch, displace])], axis=0
    )
    taps = taps_weight.reshape(rows, -1)
    if rows % 8 == 0:
        vectors = jnp.pad(vectors, ((0, 16 - KERNEL - 4), (0, 0)))
        packed, grouped = pl.pallas_call(
            pack_kernel,
            out_shape=[
                jax.ShapeDtypeStruct((rows, 5 * ATT + D + 128), LOW),
                jax.ShapeDtypeStruct((rows, 4 * D), LOW),
            ],
            name="pack",
        )(
            query_weight, key_weight, point_weight, value_weight, span_weight, output_weight,
            vectors, taps, inner_weight.swapaxes(1, 2), outer_weight,
        )
    else:
        small = jnp.pad(jnp.concatenate([vectors.T, taps], axis=1), ((0, 0), (0, 128 - used)))
        packed = jnp.concatenate(
            [
                query_weight, key_weight, point_weight, small, value_weight, span_weight,
                output_weight,
            ],
            axis=1,
        )
        grouped = jnp.concatenate(
            [outer_weight[0], outer_weight[1], inner_weight[0].T, inner_weight[1].T], axis=1
        )
        grouped = jnp.concatenate([grouped[:rows], grouped[rows:]], axis=1)
    parts = Staged(links.gather_outer(packed, (3 * ATT + 128, 2 * ATT + D))).finish()
    parts, grouped = lax.optimization_barrier((parts, grouped))
    leading = Staged(links.gather_tails([[part] for part in parts]))
    outer = Staged(links.gather_outer(grouped, (2 * D, 2 * D)))
    while not leading.ended:
        outer.value = leading.behind(outer.value)
        outer.step()
    slots = leading.finish()
    first, second = (links.owners(jnp.concatenate(slots[i], axis=0), i) for i in range(2))
    first, second, parts = lax.optimization_barrier((first, second, outer.finish()))
    gathering = Staged(links.gather_tails([[part] for part in parts]))

    (
        query, keys, values, key_conv, depthwise, mixture, tap_weights, span_values, vectors, taps,
    ) = project_call(lengths, tokens, first, second)
    query = gathering.behind(query)
    context, logsum = attend_call(lengths, query, keys, values)
    tap_weights, context = gathering.behind((tap_weights, context))
    span_output = span_call(tap_weights, span_values)
    span_output = gathering.behind(span_output)
    quarters = [piece.reshape(D // 2, 2 * D) for half in gathering.finish() for piece in half]

    (
        activations, grad_one, grad_context, grad_span, send, keep, output_grad, vector_grad,
    ) = feed_call(lengths, tokens, context, span_output, cotangent, second, quarters, vectors)
    reducing = Staged(links.reduce_slots(send, keep))
    grad_span_values, grad_mixconv, grad_conv, taps_grad = span_back_call(
        grad_span, tap_weights, span_values, mixture, query, key_conv, taps
    )
    grad_conv = reducing.behind(grad_conv)
    grad_shifted, point_grad, small_grad = depth_back_call(
        lengths, tokens, grad_conv, depthwise, first, vectors, taps_grad, vector_grad
    )
    grad_mixconv, grad_shifted = reducing.behind((grad_mixconv, grad_shifted))
    grads = []
    for index in range(tokens.shape[0]):
        arrays = [query, keys, values, logsum, grad_context, grad_mixconv]
        grads = attend_back_call(index, lengths, arrays, grads)
        grads = reducing.behind(grads)
    grad_query, grad_keys, grad_values = grads
    positions = lax.broadcasted_iota(jnp.int32, tokens.shape[:2], 1)
    masked = tokens * (positions < lengths[:, None]).astype(tokens.dtype)[..., None]
    qk_grad = weight_term(masked, jnp.concatenate([grad_query, grad_keys], axis=-1))
    vs_grad = weight_term(masked, jnp.concatenate([grad_values, grad_span_values], axis=-1))
    summing = Staged(links.reduce_owners([qk_grad, point_grad, small_grad], [vs_grad, output_grad]))
    grad_one = summing.behind(grad_one)
    tokens_grad = tokens_call(
        lengths,
        [grad_query, grad_keys, grad_values, grad_span_values, grad_one, grad_shifted],
        first,
        second,
    )
    tokens_grad = reducing.meet(tokens_grad)
    tokens_grad = summing.meet(tokens_grad)
    grouped_sum = reducing.finish().reshape(-1, 2 * D)
    summed = summing.finish()[0]
    wide = WIDE
    small_sum = summed[:, 3 * ATT : 3 * ATT + 128]
    second_sum = summed[:, 3 * ATT + 128 :]
    return (
        activations,
        tokens_grad,
        summed[:, :ATT],
        summed[:, ATT : 2 * ATT],
        second_sum[:, :ATT],
        small_sum[:, :KERNEL].T,
        summed[:, 2 * ATT : 3 * ATT],
        small_sum[:, KERNEL + 4 : used].reshape(-1),
        second_sum[:, ATT : 2 * ATT],
        second_sum[:, 2 * ATT :],
        small_sum[:, KERNEL],
        small_sum[:, KERNEL + 1],
        jnp.stack([grouped_sum[:, D + g * wide : D + (g + 1) * wide].T for g in range(GROUPS)]),
        jnp.stack([grouped_sum[:, g * wide : (g + 1) * wide] for g in range(GROUPS)]),
        small_sum[:, KERNEL + 2],
        small_sum[:, KERNEL + 3],
    )


def solution(mesh):
    both = ("dp", "fsdp")
    weights = (
        P(both, None),
        P(both, None),
        P(both, None),
        P(None, both),
        P(both, None),
        P(both),
        P(both, None),
        P(both, None),
        P(both),
        P(both),
        P(None, None, both),
        P(None, both, None),
        P(both),
        P(both),
    )
    row = P(both, None, None)
    links = Links(mesh.shape["dp"], mesh.shape["fsdp"])

    def body(*args):
        return on_device(links, *args)

    return jax.shard_map(
        body,
        mesh=mesh,
        in_specs=(row, P(both)) + weights + (row,),
        out_specs=(row, row) + weights,
        check_vma=False,
    )
```
